32 devices in a mesh: grp: 4 (over y, x), tile: 8 (over z, core).
Axes of the slice: x: 2, y: 2, z: 4, core: 2. Of those that a mesh axis runs over, the one named last changes fastest.
Arguments:
- tile_stack: bfloat16 [4, 8, 3, 8, 384, 384], P('grp', 'tile'), may hold values from 0.1 to 13
- tile_offsets: int32 [4, 8, 2], replicated, may hold values from 0 to 127, as said below
Outputs:
- joined: float32 [3, 8, 1024, 2048], P(None, None, 'grp', 'tile')
The draws below stay inside these ranges and needn't reach their ends.
Inputs may be any that keep to these rules, and one draw needn't show every extreme that they name: Tile (g, t) starts at row g * 256 + tile_offsets[g, t, 0] and column t * 256 + tile_offsets[g, t, 1] of the joined image; the row offset is 0 in grid row 0 and the column offset is 0 in grid column 0.
All inputs are finite; a program needn't handle non-finite values.
Results may differ from the reference program's by a relative error of at most 0.00041.
Values may be sent and summed in bfloat16 or wider, within the bound.
A program may use at most 256 MiB of HBM per device.

```python
import math
import jax
import jax.numpy as jnp
from jax import lax

CHANNELS = 3
PLANES = 8
TILE_EDGE = 384
JITTER = 128
BRICK_EDGE = 256
REACH = 256
CANVAS = 512
GRID_ROWS = 4
GRID_COLS = 8


def draw_tile_stack(key, part):
    key_tile, key_rows, key_cols, key_noise = jax.random.split(key, 4)
    tile_count = GRID_ROWS * GRID_COLS
    position = jnp.arange(tile_count, dtype=jnp.float32).reshape(GRID_ROWS, GRID_COLS) / max(tile_count - 1, 1)
    rising = jnp.exp(position * math.log(3.0))
    tile_level = jnp.exp(jax.random.uniform(key_tile, (GRID_ROWS, GRID_COLS, CHANNELS), jnp.float32, math.log(0.4), math.log(2.5)))
    tile_bright = rising[:, :, None] * tile_level
    row_amp = jax.random.uniform(key_rows, (GRID_ROWS, GRID_COLS, 1, PLANES, TILE_EDGE, 1), jnp.float32, 0.2, 1.0)
    col_amp = jax.random.uniform(key_cols, (GRID_ROWS, GRID_COLS, 1, PLANES, 1, TILE_EDGE), jnp.float32, 0.2, 1.0)
    amplitude = 0.05 + 0.6 * row_amp * col_amp
    full_shape = (GRID_ROWS, GRID_COLS, CHANNELS, PLANES, TILE_EDGE, TILE_EDGE)
    noise = jax.random.uniform(key_noise, full_shape, jnp.float32, -1.0, 1.0)
    values = tile_bright[:, :, :, None, None, None] * (1.0 + amplitude * noise)
    return values.astype(jnp.bfloat16)


def draw_tile_offsets(key, part):
    drawn = jax.random.randint(key, (GRID_ROWS, GRID_COLS, 2), 0, JITTER)
    row_ids = lax.broadcasted_iota(jnp.int32, (GRID_ROWS, GRID_COLS), 0)
    col_ids = lax.broadcasted_iota(jnp.int32, (GRID_ROWS, GRID_COLS), 1)
    last_tile = (row_ids == GRID_ROWS - 1) & (col_ids == GRID_COLS - 1)
    row_part = jnp.where(row_ids == 0, 0, jnp.where(last_tile, JITTER - 1, drawn[:, :, 0]))
    col_part = jnp.where(col_ids == 0, 0, jnp.where(last_tile, JITTER - 1, drawn[:, :, 1]))
    return jnp.stack([row_part, col_part], axis=-1).astype(jnp.int32)


def setup_inputs(seed: int = 0) -> dict:
    keys = jax.random.split(jax.random.key(seed), 3)
    tile_stack = draw_tile_stack(jax.random.fold_in(keys[2], 71), 0)
    tile_offsets = draw_tile_offsets(jax.random.fold_in(keys[2], 71), 0)
    return {"tile_stack": tile_stack, "tile_offsets": tile_offsets}


half_width = 7
box_area = 225.0
weight_floor = 0.1


def band_matrix(edge):
    row_ids = lax.broadcasted_iota(jnp.int32, (edge, edge), 0)
    col_ids = lax.broadcasted_iota(jnp.int32, (edge, edge), 1)
    return (jnp.abs(row_ids - col_ids) <= half_width).astype(jnp.float32)


def box_filter(values, band):
    across = jnp.einsum("cprk,kd->cprd", values, band, precision=lax.Precision.HIGHEST)
    across = lax.optimization_barrier(across.astype(jnp.bfloat16)).astype(jnp.float32)
    summed = jnp.einsum("re,cprd->cped", band, across, precision=lax.Precision.HIGHEST)
    return summed / box_area


def content_weight(tile_x):
    band = band_matrix(TILE_EDGE)
    values = tile_x.astype(jnp.float32)
    local_mean = box_filter(values, band)
    spread = (values - local_mean) * (values - local_mean)
    spread = lax.optimization_barrier(spread.astype(jnp.bfloat16)).astype(jnp.float32)
    local_var = box_filter(spread, band)
    return (weight_floor + jnp.mean(local_var, axis=0)).astype(jnp.bfloat16)


def place(tile_x, weight, row_off, col_off):
    anchor = jnp.zeros((), jnp.int32)
    row_at = row_off.astype(jnp.int32)
    col_at = col_off.astype(jnp.int32)
    canvas_x = lax.dynamic_update_slice(jnp.zeros((CHANNELS, PLANES, CANVAS, CANVAS), tile_x.dtype), tile_x, (anchor, anchor, row_at, col_at))
    canvas_w = lax.dynamic_update_slice(jnp.zeros((PLANES, CANVAS, CANVAS), weight.dtype), weight, (anchor, row_at, col_at))
    return canvas_x, canvas_w


def edge_moments(src_x, src_w, dst_x, dst_w):
    pixel_pair = src_w.astype(jnp.float32) * dst_w.astype(jnp.float32)
    source = src_x.astype(jnp.float32)
    target = dst_x.astype(jnp.float32)
    weighted_src = source * pixel_pair[None]
    weighted_dst = target * pixel_pair[None]
    axes_sum = (1, 2, 3)
    first = jnp.sum(weighted_src * source, axis=axes_sum)
    second = jnp.sum(weighted_dst * target, axis=axes_sum)
    mixed = jnp.sum(weighted_src * target, axis=axes_sum)
    src_total = jnp.sum(weighted_src, axis=axes_sum)
    dst_total = jnp.sum(weighted_dst, axis=axes_sum)
    pair_total = jnp.sum(pixel_pair) * jnp.ones_like(first)
    return jnp.stack([first, second, mixed, src_total, dst_total, pair_total])


def reference(tile_stack, tile_offsets):
    tile_count = GRID_ROWS * GRID_COLS
    flat_tiles = tile_stack.reshape(tile_count, CHANNELS, PLANES, TILE_EDGE, TILE_EDGE)
    weights = lax.map(content_weight, flat_tiles).reshape(GRID_ROWS, GRID_COLS, PLANES, TILE_EDGE, TILE_EDGE)

    def tile_canvas(row_idx, col_idx):
        is_valid = (row_idx >= 0) & (row_idx < GRID_ROWS) & (col_idx >= 0) & (col_idx < GRID_COLS)
        safe_row = jnp.clip(row_idx, 0, GRID_ROWS - 1)
        safe_col = jnp.clip(col_idx, 0, GRID_COLS - 1)
        canvas_x, canvas_w = place(tile_stack[safe_row, safe_col], weights[safe_row, safe_col], tile_offsets[safe_row, safe_col, 0], tile_offsets[safe_row, safe_col, 1])
        keep_x = is_valid.astype(canvas_x.dtype)
        keep_w = is_valid.astype(canvas_w.dtype)
        return canvas_x * keep_x, canvas_w * keep_w

    def outgoing(tile_index):
        row_idx = tile_index // GRID_COLS
        col_idx = tile_index % GRID_COLS
        own_x, own_w = tile_canvas(row_idx, col_idx)
        right_x, right_w = tile_canvas(row_idx, col_idx + 1)
        lower_x, lower_w = tile_canvas(row_idx + 1, col_idx)
        east_m = edge_moments(own_x[:, :, :, BRICK_EDGE:], own_w[:, :, BRICK_EDGE:], right_x[:, :, :, :REACH], right_w[:, :, :REACH])
        south_m = edge_moments(own_x[:, :, BRICK_EDGE:, :], own_w[:, BRICK_EDGE:, :], lower_x[:, :, :REACH, :], lower_w[:, :REACH, :])
        return east_m, south_m

    indices = jnp.arange(tile_count, dtype=jnp.int32)
    east_all, south_all = lax.map(outgoing, indices)
    east_all = east_all.reshape(GRID_ROWS, GRID_COLS, 6, CHANNELS)
    south_all = south_all.reshape(GRID_ROWS, GRID_COLS, 6, CHANNELS)
    west_all = jnp.concatenate([jnp.zeros_like(east_all[:, :1]), east_all[:, :-1]], axis=1)
    north_all = jnp.concatenate([jnp.zeros_like(south_all[:1]), south_all[:-1]], axis=0)
    own_sq = east_all[:, :, 0] + south_all[:, :, 0] + west_all[:, :, 1] + north_all[:, :, 1]
    cross = east_all[:, :, 2] + south_all[:, :, 2] + west_all[:, :, 2] + north_all[:, :, 2]
    own_sum = east_all[:, :, 3] + south_all[:, :, 3] + west_all[:, :, 4] + north_all[:, :, 4]
    other_sum = east_all[:, :, 4] + south_all[:, :, 4] + west_all[:, :, 3] + north_all[:, :, 3]
    pixel_weight = east_all[:, :, 5] + south_all[:, :, 5] + west_all[:, :, 5] + north_all[:, :, 5]
    raw_gain = cross / own_sq
    offset = (other_sum - raw_gain * own_sum) / pixel_weight
    bright = jnp.mean(tile_stack.astype(jnp.float32), axis=(3, 4, 5))
    global_scale = jnp.sum(raw_gain * bright, axis=(0, 1)) / jnp.sum(bright, axis=(0, 1))
    all_gains = raw_gain / global_scale
    all_shifts = offset / global_scale

    def weighted(piece_x, piece_w, row_idx, col_idx):
        safe_row = jnp.clip(row_idx, 0, GRID_ROWS - 1)
        safe_col = jnp.clip(col_idx, 0, GRID_COLS - 1)
        gain_now = all_gains[safe_row, safe_col][:, None, None, None]
        shift_now = all_shifts[safe_row, safe_col][:, None, None, None]
        piece_wf = piece_w.astype(jnp.float32)
        return piece_wf[None] * (gain_now * piece_x.astype(jnp.float32) + shift_now), piece_wf

    def join_brick(tile_index):
        row_idx = tile_index // GRID_COLS
        col_idx = tile_index % GRID_COLS
        own_x, own_w = tile_canvas(row_idx, col_idx)
        left_x, left_w = tile_canvas(row_idx, col_idx - 1)
        upper_x, upper_w = tile_canvas(row_idx - 1, col_idx)
        diag_x, diag_w = tile_canvas(row_idx - 1, col_idx - 1)
        numerator, denominator = weighted(own_x[:, :, :BRICK_EDGE, :BRICK_EDGE], own_w[:, :BRICK_EDGE, :BRICK_EDGE], row_idx, col_idx)
        west_num, west_den = weighted(left_x[:, :, :BRICK_EDGE, BRICK_EDGE:], left_w[:, :BRICK_EDGE, BRICK_EDGE:], row_idx, col_idx - 1)
        numerator = numerator.at[:, :, :, :REACH].add(west_num)
        denominator = denominator.at[:, :, :REACH].add(west_den)
        north_num, north_den = weighted(upper_x[:, :, BRICK_EDGE:, :BRICK_EDGE], upper_w[:, BRICK_EDGE:, :BRICK_EDGE], row_idx - 1, col_idx)
        numerator = numerator.at[:, :, :REACH, :].add(north_num)
        denominator = denominator.at[:, :REACH, :].add(north_den)
        corner_num, corner_den = weighted(diag_x[:, :, BRICK_EDGE:, BRICK_EDGE:], diag_w[:, BRICK_EDGE:, BRICK_EDGE:], row_idx - 1, col_idx - 1)
        numerator = numerator.at[:, :, :REACH, :REACH].add(corner_num)
        denominator = denominator.at[:, :REACH, :REACH].add(corner_den)
        return numerator / denominator[None]

    bricks = lax.map(join_brick, indices)
    bricks = bricks.reshape(GRID_ROWS, GRID_COLS, CHANNELS, PLANES, BRICK_EDGE, BRICK_EDGE)
    bricks = jnp.transpose(bricks, (2, 3, 0, 4, 1, 5))
    return bricks.reshape(CHANNELS, PLANES, GRID_ROWS * BRICK_EDGE, GRID_COLS * BRICK_EDGE)
```

```python
import functools

import jax
import jax.numpy as jnp
from jax import lax
from jax.experimental import pallas as pl
from jax.experimental.pallas import tpu as pltpu
from jax.sharding import PartitionSpec as P

EDGE = 384
BRICK = 256
CUT = 128
HALO = 112
STRIP = 16
AHEAD = 3
EAST_AHEAD = 3
LEAD = 3
LAG = 1
XBUF = 4
SLOTS = 6
FIRST = 144

half_width = 7
inv_area = 1.0 / 225.0
weight_floor = 0.1

BF = jnp.bfloat16
F32 = jnp.float32


def mm(a, b):
    return jnp.dot(a, b, preferred_element_type=F32)


def onehot(shape, shift):
    rows = lax.broadcasted_iota(jnp.int32, shape, 0)
    cols = lax.broadcasted_iota(jnp.int32, shape, 1)
    return (rows == cols + shift).astype(F32).astype(BF)


def onehot_cols(shape, shift):
    rows = lax.broadcasted_iota(jnp.int32, shape, 0)
    cols = lax.broadcasted_iota(jnp.int32, shape, 1)
    return (cols == rows + shift).astype(F32).astype(BF)


def band(edge):
    rows = lax.broadcasted_iota(jnp.int32, (edge, edge), 0)
    cols = lax.broadcasted_iota(jnp.int32, (edge, edge), 1)
    return (jnp.abs(rows - cols) <= half_width).astype(F32).astype(BF)


def box(x, bnd):
    r = x[0].shape[0]
    low = lax.broadcasted_iota(jnp.int32, (r, 128), 1) < 64
    cut = 192 if r == EDGE else 128
    out = []
    for v in x:
        p = mm(v[:, :256], bnd)
        q = mm(v[:, 128:], bnd)
        across = jnp.concatenate([p[:, :128], jnp.where(low, p[:, 128:], q[:, :128]), q[:, 128:]], axis=1).astype(BF)
        top = mm(bnd[:cut], across[:256])
        bottom = mm(bnd[cut - (r - 256):], across[r - 256:])
        out.append(jnp.concatenate([top, bottom], axis=0) * inv_area)
    return out


def content_weight(x, bnd):
    x = [x[i] for i in range(3)]
    mean = box(x, bnd)
    spread = []
    for i in range(3):
        d = x[i].astype(F32) - mean[i]
        spread.append((d * d).astype(BF))
    var = box(spread, bnd)
    return (weight_floor + (var[0] + var[1] + var[2]) / 3.0).astype(BF)


def put_sums(acc, base, spread=0):
    n, _, width = acc.shape
    part = jnp.sum(acc, axis=1)
    part = sum(part[:, k:k + 128] for k in range(0, width, 128))
    total = jnp.sum(part, axis=1, keepdims=True)
    lanes = lax.broadcasted_iota(jnp.int32, (n, 128), 1) - base
    here = lax.broadcasted_iota(jnp.int32, (n, 128), 0)
    mine = (lanes == here) | ((here == n - 1) & (lanes >= n) & (lanes < n + spread))
    return jnp.sum(jnp.where(mine, total, 0.0), axis=0, keepdims=True)


def fold(a):
    r, c = a.shape
    return jnp.sum(a.reshape(r // 8, 8, c), axis=0)


def add_moments(acc, src, dst):
    pi = src[3] * dst[3]
    for c in range(3):
        ws = src[c] * pi
        wd = dst[c] * pi
        acc[0 + c] += fold(ws * src[c])
        acc[3 + c] += fold(wd * dst[c])
        acc[6 + c] += fold(ws * dst[c])
        acc[9 + c] += fold(ws)
        acc[12 + c] += fold(wd)
    acc[15] += fold(pi)


def tile_kernel(
    grid_rows, grid_cols, par, x_hbm,
    own_hbm, west_hbm, north_hbm, corner_hbm, all_out,
    x, own, west, north, corner, ur,
    lr, xn, xe, we, xd, wd, w_east, w_corner, xr, wr, w_back, relay,
    bnd, put_own, put_west, put_north, put_corner, put_right,
    acc_w, acc_n, acc_d, acc_r, acc_b, row, row_buf, all_buf,
    x_sem, out_sem, sn_s, sn_r, ex_s, ex_r, ew_s, ew_r, cx_s, cx_r, cw_s, cw_r, bx_s, bx_r, bw_s, bw_r,
    rl_r, fw_s, g1_s, g1_r, g2_s, g2_r,
):
    planes = own.shape[0]
    rows = EDGE - HALO
    g, t = lax.axis_index("grp"), lax.axis_index("tile")
    has_right, has_down = t < grid_cols - 1, g < grid_rows - 1
    has_left, has_up = t > 0, g > 0
    has_diag = has_left & has_up
    is_last = g == grid_rows - 1
    gets_back, gives_back = is_last & has_right, is_last & has_left
    detours = grid_rows == 4
    to_right = {"tile": lax.rem(t + 1, grid_cols)}
    to_down = {"grp": lax.rem(g + 1, grid_rows)}
    to_left = {"tile": lax.rem(t + grid_cols - 1, grid_cols)}

    def remote(src, dst, send, recv, to):
        return pltpu.make_async_remote_copy(
            src_ref=src, dst_ref=dst, send_sem=send, recv_sem=recv, device_id=to, device_id_type=pl.DeviceIdType.MESH
        )

    def load_x(p):
        return pltpu.make_async_copy(x_hbm.at[:, p], x.at[lax.rem(p, XBUF)], x_sem.at[p])

    def send_south(p):
        return remote(x_hbm.at[:, p, pl.ds(HALO, rows), :], xn.at[p], sn_s.at[p], sn_r.at[p], to_down)

    def send_first(p):
        return remote(
            x_hbm.at[:, p, pl.ds(EDGE - FIRST, FIRST), :], xn.at[p, :, pl.ds(rows - FIRST, FIRST), :],
            sn_s.at[p], sn_r.at[p], to_down,
        )

    def send_relay(p, slot, via):
        return remote(x_hbm.at[:, p, pl.ds(HALO, rows), :], relay.at[slot], sn_s.at[p], rl_r.at[slot], {"grp": via})

    def forward(p, slot, to):
        return remote(relay.at[slot], xn.at[p], fw_s.at[slot], sn_r.at[p], {"grp": to})

    def detour(p):
        if not detours:
            return g < 0
        by_last = (g == 1) & ((p == 2) | (p == 4) | (p == 6))
        by_first = (g == 2) & ((p == 3) | (p == 5))
        return by_last | by_first

    def start_detour(slot):
        if not detours:
            return
        if slot < 3:
            @pl.when(g == 1)
            def _():
                send_relay(2 + 2 * slot, slot, 3).start()
        if slot < 2:
            @pl.when(g == 2)
            def _():
                send_relay(3 + 2 * slot, slot, 0).start()

    def pass_on(slot):
        if not detours:
            return
        if slot < 3:
            @pl.when(g == 3)
            def _():
                send_relay(2 + 2 * slot, slot, 1).wait_recv()
                forward(2 + 2 * slot, slot, 2).start()
        if slot < 2:
            @pl.when(g == 0)
            def _():
                send_relay(3 + 2 * slot, slot, 1).wait_recv()
                forward(3 + 2 * slot, slot, 3).start()

    def passed_on(slot):
        if not detours:
            return
        if slot < 3:
            @pl.when(g == 3)
            def _():
                forward(2 + 2 * slot, slot, 2).wait_send()
        if slot < 2:
            @pl.when(g == 0)
            def _():
                forward(3 + 2 * slot, slot, 3).wait_send()

    def send_back(p):
        return remote(x_hbm.at[:, p, pl.ds(CUT, BRICK), pl.ds(0, BRICK)], xr.at[p], bx_s.at[p], bx_r.at[p], to_left)

    def send_back_w(p):
        return remote(w_back.at[p], wr.at[p], bw_s.at[p], bw_r.at[p], to_left)

    def send_east(p):
        return remote(x_hbm.at[:, p, pl.ds(0, BRICK), pl.ds(CUT, BRICK)], xe.at[p], ex_s.at[p], ex_r.at[p], to_right)

    def send_east_w(p):
        return remote(w_east.at[p], we.at[p], ew_s.at[p], ew_r.at[p], to_right)

    def send_corner(p):
        return remote(
            xn.at[p, :, pl.ds(CUT - HALO, BRICK), pl.ds(CUT, BRICK)], xd.at[p], cx_s.at[p], cx_r.at[p], to_right
        )

    def send_corner_w(p):
        return remote(w_corner.at[p], wd.at[p], cw_s.at[p], cw_r.at[p], to_right)

    def store_out(k, p):
        src, dst = ((own, own_hbm), (west, west_hbm), (north, north_hbm), (corner, corner_hbm))[k]
        return pltpu.make_async_copy(src.at[p], dst.at[p], out_sem.at[k, p])

    for p in range(XBUF):
        load_x(p).start()

    barrier = pltpu.get_barrier_semaphore()
    for axis, me, size in (("tile", t, grid_cols), ("grp", g, grid_rows)):
        for d in range(1, size):
            pl.semaphore_signal(
                barrier, inc=1, device_id={axis: lax.rem(me + d, size)}, device_id_type=pl.DeviceIdType.MESH
            )
    pl.semaphore_wait(barrier, grid_cols + grid_rows - 2)

    def start_first(p):
        @pl.when(g == 0)
        def _():
            send_first(p).start()

    def start_south(p):
        @pl.when(has_down & (g > 0) & jnp.logical_not(detour(p)))
        def _():
            send_south(p).start()

    def start_east(p):
        @pl.when(has_right)
        def _():
            send_east(p).start()

    def start_back(p):
        @pl.when(gives_back)
        def _():
            send_back(p).start()

    for p in range(AHEAD):
        start_first(p)
    for p in range(planes):
        if p < 3:
            start_detour(p)
        start_south(p)
        if p < EAST_AHEAD:
            start_east(p)
        start_back(p)

    @pl.when(g == 1)
    def _():
        def clear(p, carry):
            xn[p, :, :rows - FIRST, :] = jnp.zeros((3, rows - FIRST, EDGE), BF)
            return carry

        lax.fori_loop(0, planes, clear, 0)

    def offsets(dg, dt):
        row_at, col_at = jnp.maximum(g - dg, 0), jnp.clip(t - dt, 0, grid_cols - 1)
        return par[row_at, col_at, 0], par[row_at, col_at, 1]

    bnd[...] = band(BRICK)
    for m, (dg, dt) in ((put_own, (0, 0)), (put_west, (0, 1)), (put_north, (1, 0)), (put_corner, (1, 1)), (put_right, (0, -1))):
        oy, ox = offsets(dg, dt)
        m[0] = onehot((BRICK, BRICK), oy)
        m[1] = onehot((BRICK, BRICK), oy - CUT)
        m[2] = onehot_cols((BRICK, BRICK), ox)
        m[3] = onehot_cols((BRICK, BRICK), ox - CUT)
    acc_w[...] = jnp.zeros_like(acc_w)
    acc_n[...] = jnp.zeros_like(acc_n)
    acc_d[...] = jnp.zeros_like(acc_d)
    acc_r[...] = jnp.zeros_like(acc_r)
    acc_b[...] = jnp.zeros_like(acc_b)

    def do_own(p):
        load_x(p).wait()
        v = x[lax.rem(p, XBUF)]
        w = content_weight(v, bnd[...])
        w_east[p] = w[:BRICK, CUT:]
        w_back[p] = w[CUT:, :BRICK]

        @pl.when(has_right)
        def _():
            send_east_w(p).start()

        @pl.when(gives_back)
        def _():
            send_back_w(p).start()

        slot = lax.rem(p, SLOTS)
        for c in range(4):
            a = v[c] if c < 3 else w
            if c < 3:
                acc_b[c] += fold(a.astype(F32))
            left = mm(a[:BRICK, :BRICK], put_own[2]).astype(BF)
            right = mm(a[:BRICK, CUT:], put_own[3]).astype(BF)
            own[p, c] = mm(put_own[0], left).astype(BF)
            ur[slot, c] = mm(put_own[0], right).astype(BF)

        @pl.when(gets_back)
        def _():
            for c in range(4):
                a = v[c] if c < 3 else w
                lr[slot, c] = mm(put_own[1], mm(a[CUT:, CUT:], put_own[3]).astype(BF)).astype(BF)

        store_out(0, p).start()

        @pl.when(p + XBUF < planes)
        def _():
            load_x(p + XBUF).start()

    def do_west(p):
        @pl.when(has_left)
        def _():
            send_east(p).wait_recv()
            send_east_w(p).wait_recv()
            up = []
            for c in range(4):
                a = xe[p, c] if c < 3 else we[p]
                f = mm(put_west[0], mm(a, put_west[3]).astype(BF))
                west[p, c] = f.astype(BF)
                up.append(f)
            add_moments(acc_w, up, [own[p, c].astype(F32) for c in range(4)])

        @pl.when(jnp.logical_not(has_left))
        def _():
            west[p] = jnp.zeros((4, BRICK, BRICK), BF)

        store_out(1, p).start()

    def do_north(p):
        slot = lax.rem(p, SLOTS)

        @pl.when(has_up)
        def _():
            @pl.when(g == 1)
            def _():
                send_first(p).wait_recv()

            @pl.when(g > 1)
            def _():
                send_south(p).wait_recv()

            @pl.when(has_right)
            def _():
                send_corner(p).start()

            v = xn[p]
            w = content_weight(v, bnd[...])
            w_corner[p] = w[CUT - HALO:, CUT:]

            @pl.when(has_right)
            def _():
                send_corner_w(p).start()

            left, right = [], []
            for c in range(4):
                a = v[c] if c < 3 else w
                a = a[CUT - HALO:]
                f = mm(put_north[1], mm(a[:, :BRICK], put_north[2]).astype(BF))
                north[p, c] = f.astype(BF)
                left.append(f)
                right.append(mm(put_north[1], mm(a[:, CUT:], put_north[3]).astype(BF)))
            add_moments(acc_n, left, [own[p, c].astype(F32) for c in range(4)])
            add_moments(acc_n, right, [ur[slot, c].astype(F32) for c in range(4)])

        @pl.when(jnp.logical_not(has_up))
        def _():
            north[p] = jnp.zeros((4, BRICK, BRICK), BF)

        store_out(2, p).start()

    def do_corner(p):
        @pl.when(has_diag)
        def _():
            send_corner(p).wait_recv()
            send_corner_w(p).wait_recv()
            low = []
            for c in range(4):
                a = xd[p, c] if c < 3 else wd[p]
                f = mm(put_corner[1], mm(a, put_corner[3]).astype(BF))
                corner[p, c] = f.astype(BF)
                low.append(f)
            add_moments(acc_d, low, [north[p, c].astype(F32) for c in range(4)])

        @pl.when(jnp.logical_not(has_diag))
        def _():
            corner[p] = jnp.zeros((4, BRICK, BRICK), BF)

        store_out(3, p).start()

    def do_back(p):
        slot = lax.rem(p, SLOTS)

        @pl.when(gets_back)
        def _():
            send_back(p).wait_recv()
            send_back_w(p).wait_recv()
            other = []
            for c in range(4):
                a = xr[p, c] if c < 3 else wr[p]
                other.append(mm(put_right[1], mm(a, put_right[2]).astype(BF)))
            add_moments(acc_r, [lr[slot, c].astype(F32) for c in range(4)], other)

    def step(q, carry):
        p = q - LEAD

        @pl.when(q < planes)
        def _():
            do_own(q)

            @pl.when(q + EAST_AHEAD < planes)
            def _():
                start_east(q + EAST_AHEAD)

        @pl.when((p >= 0) & (p < planes))
        def _():
            @pl.when(g == 0)
            def _():
                send_first(p).wait_send()

                @pl.when(p + AHEAD < planes)
                def _():
                    start_first(p + AHEAD)

            do_north(p)

            for k in range(3):
                @pl.when(p == k + 1)
                def _():
                    pass_on(k)


        @pl.when((p >= LAG) & (p < planes + LAG))
        def _():
            do_west(p - LAG)
            do_back(p - LAG)

        @pl.when((p >= LAG + 1) & (p < planes + LAG + 1))
        def _():
            do_corner(p - LAG - 1)

        return carry

    lax.fori_loop(0, planes + LEAD + LAG + 1, step, 0)

    total = put_sums(acc_d[...], 40, 2) + put_sums(acc_w[...], 0, 2) + put_sums(acc_n[...], 20, 2) + put_sums(acc_r[...], 60, 2) + put_sums(acc_b[...], 80)
    first = lax.broadcasted_iota(jnp.int32, (8, 128), 0) == 0
    row[...] = jnp.where(first, total, 0.0)

    def along_tile(d):
        return remote(row, row_buf.at[t], g1_s.at[d], g1_r.at[d], {"tile": lax.rem(t + d, grid_cols)})

    def along_grp(d):
        return remote(row_buf, all_buf.at[g], g2_s.at[d], g2_r.at[d], {"grp": lax.rem(g + d, grid_rows)})

    for d in range(1, grid_cols):
        along_tile(d).start()
    row_buf[t] = row[...]
    for d in range(1, grid_cols):
        along_tile(d).wait_recv()
    for d in range(1, grid_rows):
        along_grp(d).start()
    all_buf[g] = row_buf[...]
    for d in range(1, grid_rows):
        along_grp(d).wait_recv()
    all_out[...] = all_buf[...]

    for d in range(1, grid_cols):
        along_tile(d).wait_send()
    for d in range(1, grid_rows):
        along_grp(d).wait_send()

    def finish(p, carry):
        for k in range(4):
            store_out(k, p).wait()

        @pl.when(has_down & (g > 0))
        def _():
            send_south(p).wait_send()

        @pl.when(has_right)
        def _():
            send_east(p).wait_send()
            send_east_w(p).wait_send()

        @pl.when(gives_back)
        def _():
            send_back(p).wait_send()
            send_back_w(p).wait_send()

        @pl.when(has_right & has_up)
        def _():
            send_corner(p).wait_send()
            send_corner_w(p).wait_send()

        return carry

    lax.fori_loop(0, planes, finish, 0)
    for k in range(3):
        passed_on(k)


def gains(cols, all_ref, gain_ref, shift_ref):
    tiles = all_ref.shape[0]
    me = lax.axis_index("grp") * cols + lax.axis_index("tile")
    v = jnp.sum(all_ref[...], axis=1)

    def lanes_from(a, lane):
        return a if lane == 0 else pltpu.roll(a, 128 - lane, 1)

    east = pltpu.roll(v, tiles - 1, 0) + lanes_from(pltpu.roll(v, tiles - cols - 1, 0), 40) + lanes_from(v, 60)
    ahead = east + lanes_from(pltpu.roll(v, tiles - cols, 0), 20)
    behind = pltpu.roll(east, 1, 0) + lanes_from(v, 20)
    own_sq = ahead + lanes_from(behind, 3)
    cross = lanes_from(ahead + behind, 6)
    own_sum = lanes_from(ahead, 9) + lanes_from(behind, 12)
    other_sum = lanes_from(ahead, 12) + lanes_from(behind, 9)
    pixel_weight = lanes_from(ahead + behind, 15)
    bright = lanes_from(v, 80)
    raw = cross / own_sq
    off = (other_sum - raw * own_sum) / pixel_weight
    scale = jnp.sum(raw * bright, axis=0, keepdims=True) / jnp.sum(bright, axis=0, keepdims=True)
    rows = lax.broadcasted_iota(jnp.int32, (tiles, 128), 0)
    for k, back in enumerate((0, 1, cols, cols + 1)):
        here = rows == me - back
        gain_ref[k:k + 1] = jnp.sum(jnp.where(here, raw, 0.0), axis=0, keepdims=True) / scale
        shift_ref[k:k + 1] = jnp.sum(jnp.where(here, off, 0.0), axis=0, keepdims=True) / scale


def join_kernel(cols, all_ref, own, west, north, corner, out, gain_ref, shift_ref):
    @pl.when(pl.program_id(0) == 0)
    def _():
        gains(cols, all_ref, gain_ref, shift_ref)

    pieces = (own, west, north, corner)
    gain = [[jnp.broadcast_to(gain_ref[k:k + 1, c:c + 1], (STRIP, 128)) for c in range(3)] for k in range(4)]
    shift = [[jnp.broadcast_to(shift_ref[k:k + 1, c:c + 1], (STRIP, 128)) for c in range(3)] for k in range(4)]

    def strip(i, carry):
        at = pl.ds(pl.multiple_of(i * STRIP, STRIP), STRIP)
        for half in range(0, BRICK, 128):
            lanes = slice(half, half + 128)
            weights = [p[0, 3, at, lanes].astype(F32) for p in pieces]
            inv = 1.0 / (weights[0] + weights[1] + weights[2] + weights[3])
            for c in range(3):
                total = None
                for k, p in enumerate(pieces):
                    term = weights[k] * (gain[k][c] * p[0, c, at, lanes].astype(F32) + shift[k][c])
                    total = term if total is None else total + term
                out[c, 0, at, lanes] = total * inv
        return carry

    lax.fori_loop(0, BRICK // STRIP, strip, 0, unroll=2)


def local(grid_rows, grid_cols, tile_stack, tile_offsets):
    x = tile_stack[0, 0]
    planes = x.shape[1]
    rows = EDGE - HALO
    tiles = grid_rows * grid_cols
    quad = jax.ShapeDtypeStruct((planes, 4, BRICK, BRICK), BF)
    any_spec = pl.BlockSpec(memory_space=pl.ANY)

    def vmem(*shape):
        return pltpu.VMEM(shape, BF)

    def dma(*shape):
        return pltpu.SemaphoreType.DMA(shape)

    own, west, north, corner, everyone = pl.pallas_call(
        functools.partial(tile_kernel, grid_rows, grid_cols),
        out_shape=(quad,) * 4 + (jax.ShapeDtypeStruct((grid_rows, grid_cols, 8, 128), F32),),
        in_specs=[pl.BlockSpec(memory_space=pltpu.SMEM), any_spec],
        out_specs=(any_spec,) * 4 + (pl.BlockSpec(memory_space=pltpu.VMEM),),
        scratch_shapes=[vmem(XBUF, 3, EDGE, EDGE)]
        + [vmem(planes, 4, BRICK, BRICK)] * 4
        + [
            vmem(SLOTS, 4, BRICK, BRICK),
            vmem(SLOTS, 4, BRICK, BRICK),
            vmem(planes, 3, rows, EDGE),
            vmem(planes, 3, BRICK, BRICK),
            vmem(planes, BRICK, BRICK),
            vmem(planes, 3, BRICK, BRICK),
            vmem(planes, BRICK, BRICK),
            vmem(planes, BRICK, BRICK),
            vmem(planes, BRICK, BRICK),
            vmem(planes, 3, BRICK, BRICK),
            vmem(planes, BRICK, BRICK),
            vmem(planes, BRICK, BRICK),
            vmem(3, 3, rows, EDGE),
            vmem(BRICK, BRICK),
            vmem(4, BRICK, BRICK),
            vmem(4, BRICK, BRICK),
            vmem(4, BRICK, BRICK),
            vmem(4, BRICK, BRICK),
            vmem(4, BRICK, BRICK),
            pltpu.VMEM((16, 8, BRICK), F32),
            pltpu.VMEM((16, 8, BRICK), F32),
            pltpu.VMEM((16, 8, BRICK), F32),
            pltpu.VMEM((16, 8, BRICK), F32),
            pltpu.VMEM((8, 8, EDGE), F32),
            pltpu.VMEM((8, 128), F32),
            pltpu.VMEM((grid_cols, 8, 128), F32),
            pltpu.VMEM((grid_rows, grid_cols, 8, 128), F32),
            dma(planes),
            dma(4, planes),
        ]
        + [dma(planes)] * 14
        + [dma(3)] * 2
        + [dma(grid_cols)] * 2
        + [dma(grid_rows)] * 2,
        compiler_params=pltpu.CompilerParams(collective_id=0, has_side_effects=True, vmem_limit_bytes=58 << 20),
        cost_estimate=pl.CostEstimate(flops=int(4e10), bytes_accessed=int(4e7), transcendentals=0),
    )(tile_offsets, x)

    quad_spec = pl.BlockSpec((1, 4, BRICK, BRICK), lambda i: (i, 0, 0, 0))
    return pl.pallas_call(
        functools.partial(join_kernel, grid_cols),
        out_shape=jax.ShapeDtypeStruct((3, planes, BRICK, BRICK), F32),
        grid=(planes,),
        in_specs=[pl.BlockSpec((tiles, 8, 128), lambda i: (0, 0, 0))] + [quad_spec] * 4,
        out_specs=pl.BlockSpec((3, 1, BRICK, BRICK), lambda i: (0, i, 0, 0)),
        scratch_shapes=[pltpu.VMEM((8, 128), F32), pltpu.VMEM((8, 128), F32)],
        compiler_params=pltpu.CompilerParams(dimension_semantics=("arbitrary",), vmem_limit_bytes=60 << 20),
        cost_estimate=pl.CostEstimate(flops=int(1e8), bytes_accessed=int(2.3e7), transcendentals=0),
    )(everyone.reshape(tiles, 8, 128), own, west, north, corner)


def solution(mesh):
    return jax.shard_map(
        functools.partial(local, mesh.shape["grp"], mesh.shape["tile"]),
        mesh=mesh,
        in_specs=(P("grp", "tile", None, None, None, None), P()),
        out_specs=P(None, None, "grp", "tile"),
        check_vma=False,
    )
```

```python
import functools

import jax
import jax.numpy as jnp
from jax import lax
from jax.experimental import pallas as pl
from jax.experimental.pallas import tpu as pltpu
from jax.sharding import PartitionSpec as P

EDGE = 384
BRICK = 256
CUT = 128
HALO = 112
STRIP = 16
AHEAD = 3
EAST_AHEAD = 3
LEAD = 3
LAG = 1
XBUF = 4
SLOTS = 6
FIRST = 144

half_width = 7
inv_area = 1.0 / 225.0
weight_floor = 0.1

BF = jnp.bfloat16
F32 = jnp.float32


def mm(a, b):
    return jnp.dot(a, b, preferred_element_type=F32)


def onehot(shape, shift):
    rows = lax.broadcasted_iota(jnp.int32, shape, 0)
    cols = lax.broadcasted_iota(jnp.int32, shape, 1)
    return (rows == cols + shift).astype(F32).astype(BF)


def onehot_cols(shape, shift):
    rows = lax.broadcasted_iota(jnp.int32, shape, 0)
    cols = lax.broadcasted_iota(jnp.int32, shape, 1)
    return (cols == rows + shift).astype(F32).astype(BF)


def band(edge):
    rows = lax.broadcasted_iota(jnp.int32, (edge, edge), 0)
    cols = lax.broadcasted_iota(jnp.int32, (edge, edge), 1)
    return (jnp.abs(rows - cols) <= half_width).astype(F32).astype(BF)


def box(x, bnd):
    r = x[0].shape[0]
    low = lax.broadcasted_iota(jnp.int32, (r, 128), 1) < 64
    cut = 192 if r == EDGE else 128
    out = []
    for v in x:
        p = mm(v[:, :256], bnd)
        q = mm(v[:, 128:], bnd)
        across = jnp.concatenate([p[:, :128], jnp.where(low, p[:, 128:], q[:, :128]), q[:, 128:]], axis=1).astype(BF)
        top = mm(bnd[:cut], across[:256])
        bottom = mm(bnd[cut - (r - 256):], across[r - 256:])
        out.append(jnp.concatenate([top, bottom], axis=0) * inv_area)
    return out


def content_weight(x, bnd):
    x = [x[i] for i in range(3)]
    mean = box(x, bnd)
    spread = []
    for i in range(3):
        d = x[i].astype(F32) - mean[i]
        spread.append((d * d).astype(BF))
    var = box(spread, bnd)
    return (weight_floor + (var[0] + var[1] + var[2]) / 3.0).astype(BF)


def put_sums(acc, base, spread=0):
    n, _, width = acc.shape
    part = jnp.sum(acc, axis=1)
    part = sum(part[:, k:k + 128] for k in range(0, width, 128))
    total = jnp.sum(part, axis=1, keepdims=True)
    lanes = lax.broadcasted_iota(jnp.int32, (n, 128), 1) - base
    here = lax.broadcasted_iota(jnp.int32, (n, 128), 0)
    mine = (lanes == here) | ((here == n - 1) & (lanes >= n) & (lanes < n + spread))
    return jnp.sum(jnp.where(mine, total, 0.0), axis=0, keepdims=True)


def fold(a):
    r, c = a.shape
    return jnp.sum(a.reshape(r // 8, 8, c), axis=0)


def add_moments(acc, src, dst):
    pi = src[3] * dst[3]
    for c in range(3):
        ws = src[c] * pi
        wd = dst[c] * pi
        acc[0 + c] += fold(ws * src[c])
        acc[3 + c] += fold(wd * dst[c])
        acc[6 + c] += fold(ws * dst[c])
        acc[9 + c] += fold(ws)
        acc[12 + c] += fold(wd)
    acc[15] += fold(pi)


def tile_kernel(
    grid_rows, grid_cols, par, x_hbm,
    own, west, north, corner, all_out,
    x, ur,
    lr, xn, xe, we, xd, wd, w_east, w_corner, xr, wr, w_back, relay,
    bnd, put_own, put_west, put_north, put_corner, put_right,
    acc_w, acc_n, acc_d, acc_r, acc_b, row, row_buf, all_buf,
    x_sem, sn_s, sn_r, ex_s, ex_r, ew_s, ew_r, cx_s, cx_r, cw_s, cw_r, bx_s, bx_r, bw_s, bw_r,
    rl_r, fw_s, g1_s, g1_r, g2_s, g2_r,
):
    planes = own.shape[0]
    rows = EDGE - HALO
    g, t = lax.axis_index("grp"), lax.axis_index("tile")
    has_right, has_down = t < grid_cols - 1, g < grid_rows - 1
    has_left, has_up = t > 0, g > 0
    has_diag = has_left & has_up
    is_last = g == grid_rows - 1
    gets_back, gives_back = is_last & has_right, is_last & has_left
    detours = grid_rows == 4
    to_right = {"tile": lax.rem(t + 1, grid_cols)}
    to_down = {"grp": lax.rem(g + 1, grid_rows)}
    to_left = {"tile": lax.rem(t + grid_cols - 1, grid_cols)}

    def remote(src, dst, send, recv, to):
        return pltpu.make_async_remote_copy(
            src_ref=src, dst_ref=dst, send_sem=send, recv_sem=recv, device_id=to, device_id_type=pl.DeviceIdType.MESH
        )

    def load_x(p):
        return pltpu.make_async_copy(x_hbm.at[:, p], x.at[lax.rem(p, XBUF)], x_sem.at[p])

    def send_south(p):
        return remote(x_hbm.at[:, p, pl.ds(HALO, rows), :], xn.at[p], sn_s.at[p], sn_r.at[p], to_down)

    def send_first(p):
        return remote(
            x_hbm.at[:, p, pl.ds(EDGE - FIRST, FIRST), :], xn.at[p, :, pl.ds(rows - FIRST, FIRST), :],
            sn_s.at[p], sn_r.at[p], to_down,
        )

    def send_relay(p, slot, via):
        return remote(x_hbm.at[:, p, pl.ds(HALO, rows), :], relay.at[slot], sn_s.at[p], rl_r.at[slot], {"grp": via})

    def forward(p, slot, to):
        return remote(relay.at[slot], xn.at[p], fw_s.at[slot], sn_r.at[p], {"grp": to})

    def detour(p):
        if not detours:
            return g < 0
        by_last = (g == 1) & ((p == 2) | (p == 4) | (p == 6))
        by_first = (g == 2) & ((p == 3) | (p == 5))
        return by_last | by_first

    def start_detour(slot):
        if not detours:
            return
        if slot < 3:
            @pl.when(g == 1)
            def _():
                send_relay(2 + 2 * slot, slot, 3).start()
        if slot < 2:
            @pl.when(g == 2)
            def _():
                send_relay(3 + 2 * slot, slot, 0).start()

    def pass_on(slot):
        if not detours:
            return
        if slot < 3:
            @pl.when(g == 3)
            def _():
                send_relay(2 + 2 * slot, slot, 1).wait_recv()
                forward(2 + 2 * slot, slot, 2).start()
        if slot < 2:
            @pl.when(g == 0)
            def _():
                send_relay(3 + 2 * slot, slot, 1).wait_recv()
                forward(3 + 2 * slot, slot, 3).start()

    def passed_on(slot):
        if not detours:
            return
        if slot < 3:
            @pl.when(g == 3)
            def _():
                forward(2 + 2 * slot, slot, 2).wait_send()
        if slot < 2:
            @pl.when(g == 0)
            def _():
                forward(3 + 2 * slot, slot, 3).wait_send()

    def send_back(p):
        return remote(x_hbm.at[:, p, pl.ds(CUT, BRICK), pl.ds(0, BRICK)], xr.at[p], bx_s.at[p], bx_r.at[p], to_left)

    def send_back_w(p):
        return remote(w_back.at[p], wr.at[p], bw_s.at[p], bw_r.at[p], to_left)

    def send_east(p):
        return remote(x_hbm.at[:, p, pl.ds(0, BRICK), pl.ds(CUT, BRICK)], xe.at[p], ex_s.at[p], ex_r.at[p], to_right)

    def send_east_w(p):
        return remote(w_east.at[p], we.at[p], ew_s.at[p], ew_r.at[p], to_right)

    def send_corner(p):
        return remote(
            xn.at[p, :, pl.ds(CUT - HALO, BRICK), pl.ds(CUT, BRICK)], xd.at[p], cx_s.at[p], cx_r.at[p], to_right
        )

    def send_corner_w(p):
        return remote(w_corner.at[p], wd.at[p], cw_s.at[p], cw_r.at[p], to_right)

    for p in range(XBUF):
        load_x(p).start()

    barrier = pltpu.get_barrier_semaphore()
    for axis, me, size in (("tile", t, grid_cols), ("grp", g, grid_rows)):
        for d in range(1, size):
            pl.semaphore_signal(
                barrier, inc=1, device_id={axis: lax.rem(me + d, size)}, device_id_type=pl.DeviceIdType.MESH
            )
    pl.semaphore_wait(barrier, grid_cols + grid_rows - 2)

    def start_first(p):
        @pl.when(g == 0)
        def _():
            send_first(p).start()

    def start_south(p):
        @pl.when(has_down & (g > 0) & jnp.logical_not(detour(p)))
        def _():
            send_south(p).start()

    def start_east(p):
        @pl.when(has_right)
        def _():
            send_east(p).start()

    def start_back(p):
        @pl.when(gives_back)
        def _():
            send_back(p).start()

    for p in range(AHEAD):
        start_first(p)
    for p in range(planes):
        if p < 3:
            start_detour(p)
        start_south(p)
        if p < EAST_AHEAD:
            start_east(p)
        start_back(p)

    @pl.when(g == 1)
    def _():
        def clear(p, carry):
            xn[p, :, :rows - FIRST, :] = jnp.zeros((3, rows - FIRST, EDGE), BF)
            return carry

        lax.fori_loop(0, planes, clear, 0)

    def offsets(dg, dt):
        row_at, col_at = jnp.maximum(g - dg, 0), jnp.clip(t - dt, 0, grid_cols - 1)
        return par[row_at, 0, col_at], par[row_at, 1, col_at]

    bnd[...] = band(BRICK)
    for m, (dg, dt) in ((put_own, (0, 0)), (put_west, (0, 1)), (put_north, (1, 0)), (put_corner, (1, 1)), (put_right, (0, -1))):
        oy, ox = offsets(dg, dt)
        m[0] = onehot((BRICK, BRICK), oy)
        m[1] = onehot((BRICK, BRICK), oy - CUT)
        m[2] = onehot_cols((BRICK, BRICK), ox)
        m[3] = onehot_cols((BRICK, BRICK), ox - CUT)
    acc_w[...] = jnp.zeros_like(acc_w)
    acc_n[...] = jnp.zeros_like(acc_n)
    acc_d[...] = jnp.zeros_like(acc_d)
    acc_r[...] = jnp.zeros_like(acc_r)
    acc_b[...] = jnp.zeros_like(acc_b)

    def do_own(p):
        load_x(p).wait()
        v = x[lax.rem(p, XBUF)]
        w = content_weight(v, bnd[...])
        w_east[p] = w[:BRICK, CUT:]
        w_back[p] = w[CUT:, :BRICK]

        @pl.when(has_right)
        def _():
            send_east_w(p).start()

        @pl.when(gives_back)
        def _():
            send_back_w(p).start()

        slot = lax.rem(p, SLOTS)
        for c in range(4):
            a = v[c] if c < 3 else w
            if c < 3:
                acc_b[c] += fold(a.astype(F32))
            left = mm(a[:BRICK, :BRICK], put_own[2]).astype(BF)
            right = mm(a[:BRICK, CUT:], put_own[3]).astype(BF)
            own[p, c] = mm(put_own[0], left).astype(BF)
            ur[slot, c] = mm(put_own[0], right).astype(BF)

        @pl.when(gets_back)
        def _():
            for c in range(4):
                a = v[c] if c < 3 else w
                lr[slot, c] = mm(put_own[1], mm(a[CUT:, CUT:], put_own[3]).astype(BF)).astype(BF)


        @pl.when(p + XBUF < planes)
        def _():
            load_x(p + XBUF).start()

    def do_west(p):
        @pl.when(has_left)
        def _():
            send_east(p).wait_recv()
            send_east_w(p).wait_recv()
            up = []
            for c in range(4):
                a = xe[p, c] if c < 3 else we[p]
                f = mm(put_west[0], mm(a, put_west[3]).astype(BF))
                west[p, c] = f.astype(BF)
                up.append(f)
            add_moments(acc_w, up, [own[p, c].astype(F32) for c in range(4)])

        @pl.when(jnp.logical_not(has_left))
        def _():
            west[p] = jnp.zeros((4, BRICK, BRICK), BF)


    def do_north(p):
        slot = lax.rem(p, SLOTS)

        @pl.when(has_up)
        def _():
            @pl.when(g == 1)
            def _():
                send_first(p).wait_recv()

            @pl.when(g > 1)
            def _():
                send_south(p).wait_recv()

            @pl.when(has_right)
            def _():
                send_corner(p).start()

            v = xn[p]
            w = content_weight(v, bnd[...])
            w_corner[p] = w[CUT - HALO:, CUT:]

            @pl.when(has_right)
            def _():
                send_corner_w(p).start()

            left, right = [], []
            for c in range(4):
                a = v[c] if c < 3 else w
                a = a[CUT - HALO:]
                f = mm(put_north[1], mm(a[:, :BRICK], put_north[2]).astype(BF))
                north[p, c] = f.astype(BF)
                left.append(f)
                right.append(mm(put_north[1], mm(a[:, CUT:], put_north[3]).astype(BF)))
            add_moments(acc_n, left, [own[p, c].astype(F32) for c in range(4)])
            add_moments(acc_n, right, [ur[slot, c].astype(F32) for c in range(4)])

        @pl.when(jnp.logical_not(has_up))
        def _():
            north[p] = jnp.zeros((4, BRICK, BRICK), BF)


    def do_corner(p):
        @pl.when(has_diag)
        def _():
            send_corner(p).wait_recv()
            send_corner_w(p).wait_recv()
            low = []
            for c in range(4):
                a = xd[p, c] if c < 3 else wd[p]
                f = mm(put_corner[1], mm(a, put_corner[3]).astype(BF))
                corner[p, c] = f.astype(BF)
                low.append(f)
            add_moments(acc_d, low, [north[p, c].astype(F32) for c in range(4)])

        @pl.when(jnp.logical_not(has_diag))
        def _():
            corner[p] = jnp.zeros((4, BRICK, BRICK), BF)


    def do_back(p):
        slot = lax.rem(p, SLOTS)

        @pl.when(gets_back)
        def _():
            send_back(p).wait_recv()
            send_back_w(p).wait_recv()
            other = []
            for c in range(4):
                a = xr[p, c] if c < 3 else wr[p]
                other.append(mm(put_right[1], mm(a, put_right[2]).astype(BF)))
            add_moments(acc_r, [lr[slot, c].astype(F32) for c in range(4)], other)

    def step(q, carry):
        p = q - LEAD

        @pl.when(q < planes)
        def _():
            do_own(q)

            @pl.when(q + EAST_AHEAD < planes)
            def _():
                start_east(q + EAST_AHEAD)

        @pl.when((p >= 0) & (p < planes))
        def _():
            @pl.when(g == 0)
            def _():
                send_first(p).wait_send()

                @pl.when(p + AHEAD < planes)
                def _():
                    start_first(p + AHEAD)

            do_north(p)

            for k in range(3):
                @pl.when(p == k + 1)
                def _():
                    pass_on(k)


        @pl.when((p >= LAG) & (p < planes + LAG))
        def _():
            do_west(p - LAG)
            do_back(p - LAG)

        @pl.when((p >= LAG + 1) & (p < planes + LAG + 1))
        def _():
            do_corner(p - LAG - 1)

        return carry

    lax.fori_loop(0, planes + LEAD + LAG + 1, step, 0)

    total = put_sums(acc_d[...], 40, 2) + put_sums(acc_w[...], 0, 2) + put_sums(acc_n[...], 20, 2) + put_sums(acc_r[...], 60, 2) + put_sums(acc_b[...], 80)
    first = lax.broadcasted_iota(jnp.int32, (8, 128), 0) == 0
    row[...] = jnp.where(first, total, 0.0)

    def along_tile(d):
        return remote(row, row_buf.at[t], g1_s.at[d], g1_r.at[d], {"tile": lax.rem(t + d, grid_cols)})

    def along_grp(d):
        return remote(row_buf, all_buf.at[g], g2_s.at[d], g2_r.at[d], {"grp": lax.rem(g + d, grid_rows)})

    for d in range(1, grid_cols):
        along_tile(d).start()
    row_buf[t] = row[...]
    for d in range(1, grid_cols):
        along_tile(d).wait_recv()
    for d in range(1, grid_rows):
        along_grp(d).start()
    all_buf[g] = row_buf[...]
    for d in range(1, grid_rows):
        along_grp(d).wait_recv()
    all_out[...] = all_buf[...]

    for d in range(1, grid_cols):
        along_tile(d).wait_send()
    for d in range(1, grid_rows):
        along_grp(d).wait_send()

    def finish(p, carry):
        @pl.when(has_down & (g > 0))
        def _():
            send_south(p).wait_send()

        @pl.when(has_right)
        def _():
            send_east(p).wait_send()
            send_east_w(p).wait_send()

        @pl.when(gives_back)
        def _():
            send_back(p).wait_send()
            send_back_w(p).wait_send()

        @pl.when(has_right & has_up)
        def _():
            send_corner(p).wait_send()
            send_corner_w(p).wait_send()

        return carry

    lax.fori_loop(0, planes, finish, 0)
    for k in range(3):
        passed_on(k)


def gains(cols, all_ref, gain_ref, shift_ref):
    tiles = all_ref.shape[0]
    me = lax.axis_index("grp") * cols + lax.axis_index("tile")
    v = jnp.sum(all_ref[...], axis=1)

    def lanes_from(a, lane):
        return a if lane == 0 else pltpu.roll(a, 128 - lane, 1)

    east = pltpu.roll(v, tiles - 1, 0) + lanes_from(pltpu.roll(v, tiles - cols - 1, 0), 40) + lanes_from(v, 60)
    ahead = east + lanes_from(pltpu.roll(v, tiles - cols, 0), 20)
    behind = pltpu.roll(east, 1, 0) + lanes_from(v, 20)
    own_sq = ahead + lanes_from(behind, 3)
    cross = lanes_from(ahead + behind, 6)
    own_sum = lanes_from(ahead, 9) + lanes_from(behind, 12)
    other_sum = lanes_from(ahead, 12) + lanes_from(behind, 9)
    pixel_weight = lanes_from(ahead + behind, 15)
    bright = lanes_from(v, 80)
    raw = cross / own_sq
    off = (other_sum - raw * own_sum) / pixel_weight
    scale = jnp.sum(raw * bright, axis=0, keepdims=True) / jnp.sum(bright, axis=0, keepdims=True)
    rows = lax.broadcasted_iota(jnp.int32, (tiles, 128), 0)
    for k, back in enumerate((0, 1, cols, cols + 1)):
        here = rows == me - back
        gain_ref[k:k + 1] = jnp.sum(jnp.where(here, raw, 0.0), axis=0, keepdims=True) / scale
        shift_ref[k:k + 1] = jnp.sum(jnp.where(here, off, 0.0), axis=0, keepdims=True) / scale


def join_kernel(cols, all_ref, own, west, north, corner, out, gain_ref, shift_ref):
    p = pl.program_id(0)

    @pl.when(p == 0)
    def _():
        gains(cols, all_ref, gain_ref, shift_ref)

    pieces = (own, west, north, corner)
    gain = [[jnp.broadcast_to(gain_ref[k:k + 1, c:c + 1], (STRIP, 128)) for c in range(3)] for k in range(4)]
    shift = [[jnp.broadcast_to(shift_ref[k:k + 1, c:c + 1], (STRIP, 128)) for c in range(3)] for k in range(4)]

    def strip(i, carry):
        at = pl.ds(pl.multiple_of(i * STRIP, STRIP), STRIP)
        for half in range(0, BRICK, 128):
            lanes = slice(half, half + 128)
            weights = [a[p, 3, at, lanes].astype(F32) for a in pieces]
            inv = 1.0 / (weights[0] + weights[1] + weights[2] + weights[3])
            for c in range(3):
                total = None
                for k, a in enumerate(pieces):
                    term = weights[k] * (gain[k][c] * a[p, c, at, lanes].astype(F32) + shift[k][c])
                    total = term if total is None else total + term
                out[c, 0, at, lanes] = total * inv
        return carry

    lax.fori_loop(0, BRICK // STRIP, strip, 0, unroll=2)


def local(grid_rows, grid_cols, tile_stack, tile_offsets):
    x = tile_stack[0, 0]
    planes = x.shape[1]
    rows = EDGE - HALO
    tiles = grid_rows * grid_cols
    quad = pltpu.VMEM((planes, 4, BRICK, BRICK), BF)
    vmem_spec = pl.BlockSpec(memory_space=pltpu.VMEM)
    any_spec = pl.BlockSpec(memory_space=pl.ANY)

    def vmem(*shape):
        return pltpu.VMEM(shape, BF)

    def dma(*shape):
        return pltpu.SemaphoreType.DMA(shape)

    own, west, north, corner, everyone = pl.pallas_call(
        functools.partial(tile_kernel, grid_rows, grid_cols),
        out_shape=(quad,) * 4 + (pltpu.VMEM((grid_rows, grid_cols, 8, 128), F32),),
        in_specs=[pl.BlockSpec(memory_space=pltpu.SMEM), any_spec],
        out_specs=(vmem_spec,) * 5,
        scratch_shapes=[vmem(XBUF, 3, EDGE, EDGE)]
        + [
            vmem(SLOTS, 4, BRICK, BRICK),
            vmem(SLOTS, 4, BRICK, BRICK),
            vmem(planes, 3, rows, EDGE),
            vmem(planes, 3, BRICK, BRICK),
            vmem(planes, BRICK, BRICK),
            vmem(planes, 3, BRICK, BRICK),
            vmem(planes, BRICK, BRICK),
            vmem(planes, BRICK, BRICK),
            vmem(planes, BRICK, BRICK),
            vmem(planes, 3, BRICK, BRICK),
            vmem(planes, BRICK, BRICK),
            vmem(planes, BRICK, BRICK),
            vmem(3, 3, rows, EDGE),
            vmem(BRICK, BRICK),
            vmem(4, BRICK, BRICK),
            vmem(4, BRICK, BRICK),
            vmem(4, BRICK, BRICK),
            vmem(4, BRICK, BRICK),
            vmem(4, BRICK, BRICK),
            pltpu.VMEM((16, 8, BRICK), F32),
            pltpu.VMEM((16, 8, BRICK), F32),
            pltpu.VMEM((16, 8, BRICK), F32),
            pltpu.VMEM((16, 8, BRICK), F32),
            pltpu.VMEM((8, 8, EDGE), F32),
            pltpu.VMEM((8, 128), F32),
            pltpu.VMEM((grid_cols, 8, 128), F32),
            pltpu.VMEM((grid_rows, grid_cols, 8, 128), F32),
            dma(planes),
        ]
        + [dma(planes)] * 14
        + [dma(3)] * 2
        + [dma(grid_cols)] * 2
        + [dma(grid_rows)] * 2,
        compiler_params=pltpu.CompilerParams(collective_id=0, has_side_effects=True, vmem_limit_bytes=42 << 20),
        cost_estimate=pl.CostEstimate(flops=int(4e10), bytes_accessed=int(4e7), transcendentals=0),
    )(jnp.swapaxes(tile_offsets, 1, 2), x)

    return pl.pallas_call(
        functools.partial(join_kernel, grid_cols),
        out_shape=jax.ShapeDtypeStruct((3, planes, BRICK, BRICK), F32),
        grid=(planes,),
        in_specs=[vmem_spec] * 5,
        out_specs=pl.BlockSpec((3, 1, BRICK, BRICK), lambda i: (0, i, 0, 0)),
        scratch_shapes=[pltpu.VMEM((8, 128), F32), pltpu.VMEM((8, 128), F32)],
        compiler_params=pltpu.CompilerParams(dimension_semantics=("arbitrary",), vmem_limit_bytes=16 << 20),
        cost_estimate=pl.CostEstimate(flops=int(1e8), bytes_accessed=int(2.3e7), transcendentals=0),
    )(everyone.reshape(tiles, 8, 128), own, west, north, corner)


def solution(mesh):
    return jax.shard_map(
        functools.partial(local, mesh.shape["grp"], mesh.shape["tile"]),
        mesh=mesh,
        in_specs=(P("grp", "tile", None, None, None, None), P()),
        out_specs=P(None, None, "grp", "tile"),
        check_vma=False,
    )
```

```python
import functools

import jax
import jax.numpy as jnp
from jax import lax
from jax.experimental import pallas as pl
from jax.experimental.pallas import tpu as pltpu
from jax.sharding import PartitionSpec as P

EDGE = 384
BRICK = 256
CUT = 128
TOP = 16
STRIP = 16
VIA = 3
EAST_AHEAD = 3
LEAD = 3
LAG = 1
XBUF = 4
SLOTS = 6
FIRST = 128

half_width = 7
inv_area = 1.0 / 225.0
weight_floor = 0.1

BF = jnp.bfloat16
F32 = jnp.float32


def mm(a, b):
    return jnp.dot(a, b, preferred_element_type=F32)


def onehot(shape, shift):
    rows = lax.broadcasted_iota(jnp.int32, shape, 0)
    cols = lax.broadcasted_iota(jnp.int32, shape, 1)
    return (rows == cols + shift).astype(F32).astype(BF)


def onehot_cols(shape, shift):
    rows = lax.broadcasted_iota(jnp.int32, shape, 0)
    cols = lax.broadcasted_iota(jnp.int32, shape, 1)
    return (cols == rows + shift).astype(F32).astype(BF)


def band(edge):
    rows = lax.broadcasted_iota(jnp.int32, (edge, edge), 0)
    cols = lax.broadcasted_iota(jnp.int32, (edge, edge), 1)
    return (jnp.abs(rows - cols) <= half_width).astype(F32).astype(BF)


def box(x, bnd):
    r = x[0].shape[0]
    low = lax.broadcasted_iota(jnp.int32, (r, 128), 1) < 64
    out = []
    for v in x:
        p = mm(v[:, :256], bnd)
        q = mm(v[:, 128:], bnd)
        across = jnp.concatenate([p[:, :128], jnp.where(low, p[:, 128:], q[:, :128]), q[:, 128:]], axis=1).astype(BF)
        if r == 256:
            out.append(mm(bnd, across) * inv_area)
            continue
        top = mm(bnd[:192], across[:256])
        bottom = mm(bnd[64:], across[128:])
        out.append(jnp.concatenate([top, bottom], axis=0) * inv_area)
    return out


def content_weight(x, bnd):
    x = [x[i] for i in range(3)]
    mean = box(x, bnd)
    spread = []
    for i in range(3):
        d = x[i].astype(F32) - mean[i]
        spread.append((d * d).astype(BF))
    var = box(spread, bnd)
    return (weight_floor + (var[0] + var[1] + var[2]) / 3.0).astype(BF)


def put_sums(acc, base, spread=0):
    n, _, width = acc.shape
    part = jnp.sum(acc, axis=1)
    part = sum(part[:, k:k + 128] for k in range(0, width, 128))
    total = jnp.sum(part, axis=1, keepdims=True)
    lanes = lax.broadcasted_iota(jnp.int32, (n, 128), 1) - base
    here = lax.broadcasted_iota(jnp.int32, (n, 128), 0)
    mine = (lanes == here) | ((here == n - 1) & (lanes >= n) & (lanes < n + spread))
    return jnp.sum(jnp.where(mine, total, 0.0), axis=0, keepdims=True)


def fold(a):
    r, c = a.shape
    return jnp.sum(a.reshape(r // 8, 8, c), axis=0)


def add_moments(acc, src, dst):
    pi = src[3] * dst[3]
    for c in range(3):
        ws = src[c] * pi
        wd = dst[c] * pi
        acc[0 + c] += fold(ws * src[c])
        acc[3 + c] += fold(wd * dst[c])
        acc[6 + c] += fold(ws * dst[c])
        acc[9 + c] += fold(ws)
        acc[12 + c] += fold(wd)
    acc[15] += fold(pi)


def tile_kernel(
    grid_rows, grid_cols, par, x_hbm,
    own, west, north, corner, all_out,
    x, ur,
    lr, xn, w_top, wt, wn, relay_e, xe, we, xd, wd, w_east, w_corner, xr, wr, w_back, relay,
    bnd, put_own, put_west, put_north, put_corner, put_right,
    acc_w, acc_n, acc_d, acc_r, acc_b, row, row_buf, all_buf,
    x_sem, sn_s, sn_r, ex_s, ex_r, ew_s, ew_r, cx_s, cx_r, cw_s, cw_r, bx_s, bx_r, bw_s, bw_r,
    rl_r, fw_s, tp_s, tp_r, re_r, fe_s, g1_s, g1_r, g2_s, g2_r,
):
    planes = own.shape[0]
    rows = EDGE - CUT
    g, t = lax.axis_index("grp"), lax.axis_index("tile")
    has_right, has_down = t < grid_cols - 1, g < grid_rows - 1
    has_left, has_up = t > 0, g > 0
    has_diag = has_left & has_up
    is_last = g == grid_rows - 1
    gets_back, gives_back = is_last & has_right, is_last & has_left
    detours = grid_rows == 4
    to_right = {"tile": lax.rem(t + 1, grid_cols)}
    to_down = {"grp": lax.rem(g + 1, grid_rows)}
    to_left = {"tile": lax.rem(t + grid_cols - 1, grid_cols)}

    def remote(src, dst, send, recv, to):
        return pltpu.make_async_remote_copy(
            src_ref=src, dst_ref=dst, send_sem=send, recv_sem=recv, device_id=to, device_id_type=pl.DeviceIdType.MESH
        )

    def load_x(p):
        return pltpu.make_async_copy(x_hbm.at[:, p], x.at[lax.rem(p, XBUF)], x_sem.at[p])

    def send_south(p):
        return remote(x_hbm.at[:, p, pl.ds(CUT, rows), :], xn.at[p], sn_s.at[p], sn_r.at[p], to_down)

    def send_first(p):
        return remote(
            x_hbm.at[:, p, pl.ds(EDGE - FIRST, FIRST), :], xn.at[p, :, pl.ds(rows - FIRST, FIRST), :],
            sn_s.at[p], sn_r.at[p], to_down,
        )

    def send_relay(p, slot, via):
        return remote(x_hbm.at[:, p, pl.ds(CUT, rows), :], relay.at[slot], sn_s.at[p], rl_r.at[slot], {"grp": via})

    def forward(p, slot, to):
        return remote(relay.at[slot], xn.at[p], fw_s.at[slot], sn_r.at[p], {"grp": to})

    def detour(p):
        if not detours:
            return g < 0
        by_last = (g == 1) & ((p == 2) | (p == 4) | (p == 6))
        by_first = (g == 2) & ((p == 4) | (p == 6))
        return by_last | by_first

    def start_detour(slot):
        if not detours:
            return
        if slot < 3:
            @pl.when(g == 1)
            def _():
                send_relay(2 + 2 * slot, slot, 3).start()
        if slot < 2:
            @pl.when(g == 2)
            def _():
                send_relay(4 + 2 * slot, slot, 0).start()

    def pass_on(slot):
        if not detours:
            return
        if slot < 3:
            @pl.when(g == 3)
            def _():
                send_relay(2 + 2 * slot, slot, 1).wait_recv()
                forward(2 + 2 * slot, slot, 2).start()
        if slot < 2:
            @pl.when(g == 0)
            def _():
                send_relay(4 + 2 * slot, slot, 1).wait_recv()
                forward(4 + 2 * slot, slot, 3).start()

    def passed_on(slot):
        if not detours:
            return
        if slot < 3:
            @pl.when(g == 3)
            def _():
                forward(2 + 2 * slot, slot, 2).wait_send()
        if slot < 2:
            @pl.when(g == 0)
            def _():
                forward(4 + 2 * slot, slot, 3).wait_send()

    def send_back(p):
        return remote(x_hbm.at[:, p, pl.ds(CUT, BRICK), pl.ds(0, BRICK)], xr.at[p], bx_s.at[p], bx_r.at[p], to_left)

    def send_back_w(p):
        return remote(w_back.at[p], wr.at[p], bw_s.at[p], bw_r.at[p], to_left)

    def send_east(p):
        return remote(x_hbm.at[:, p, pl.ds(0, BRICK), pl.ds(CUT, BRICK)], xe.at[p], ex_s.at[p], ex_r.at[p], to_right)

    def send_east_w(p):
        return remote(w_east.at[p], we.at[p], ew_s.at[p], ew_r.at[p], to_right)

    def send_corner(p):
        return remote(xn.at[p, :, :, pl.ds(CUT, BRICK)], xd.at[p], cx_s.at[p], cx_r.at[p], to_right)

    def send_corner_w(p):
        return remote(w_corner.at[p], wd.at[p], cw_s.at[p], cw_r.at[p], to_right)

    def send_corner_low(p):
        low = pl.ds(rows - FIRST, FIRST)
        return remote(xn.at[p, :, low, pl.ds(CUT, BRICK)], xd.at[p, :, low, :], cx_s.at[p], cx_r.at[p], to_right)

    def send_corner_w_low(p):
        low = pl.ds(rows - FIRST, FIRST)
        return remote(w_corner.at[p, low, :], wd.at[p, low, :], cw_s.at[p], cw_r.at[p], to_right)

    def corner_copies(p, act):
        @pl.when(g == 1)
        def _():
            act(send_corner_low(p))

        @pl.when(g > 1)
        def _():
            act(send_corner(p))

    def corner_w_copies(p, act):
        @pl.when(g == 1)
        def _():
            act(send_corner_w_low(p))

        @pl.when(g > 1)
        def _():
            act(send_corner_w(p))

    def send_top(p):
        return remote(w_top.at[p], wt.at[p], tp_s.at[p], tp_r.at[p], to_down)

    crosses = (lax.rem(t, 2) == 1) & has_right
    far_east = crosses & (g >= 2) if detours else t < 0
    lends = (lax.rem(t, 2) == 0) & has_left & (g < 2) if detours else g < 0
    two_rows = lax.rem(g + 2, grid_rows)

    def send_east_relay(k):
        p = planes - VIA + k
        return remote(
            x_hbm.at[:, p, pl.ds(0, BRICK), pl.ds(CUT, BRICK)], relay_e.at[k], ex_s.at[p], re_r.at[k],
            {"grp": two_rows, "tile": lax.rem(t + 1, grid_cols)},
        )

    def forward_east(k):
        p = planes - VIA + k
        return remote(relay_e.at[k], xe.at[p], fe_s.at[k], ex_r.at[p], {"grp": two_rows})

    for p in range(XBUF):
        load_x(p).start()

    barrier = pltpu.get_barrier_semaphore()
    for axis, me, size in (("tile", t, grid_cols), ("grp", g, grid_rows)):
        for d in range(1, size):
            pl.semaphore_signal(
                barrier, inc=1, device_id={axis: lax.rem(me + d, size)}, device_id_type=pl.DeviceIdType.MESH
            )

    @pl.when(lends)
    def _():
        pl.semaphore_signal(
            barrier, inc=1, device_id={"grp": two_rows, "tile": lax.rem(t + grid_cols - 1, grid_cols)},
            device_id_type=pl.DeviceIdType.MESH,
        )

    @pl.when(far_east)
    def _():
        pl.semaphore_wait(barrier, grid_cols + grid_rows - 1)

    @pl.when(jnp.logical_not(far_east))
    def _():
        pl.semaphore_wait(barrier, grid_cols + grid_rows - 2)

    def start_first(p):
        @pl.when(g == 0)
        def _():
            send_first(p).start()

    def start_south(p):
        @pl.when(has_down & (g > 0) & jnp.logical_not(detour(p)))
        def _():
            send_south(p).start()

    def start_east(p):
        @pl.when(has_right & jnp.logical_not(far_east & (p >= planes - VIA)))
        def _():
            send_east(p).start()

    def start_back(p):
        @pl.when(gives_back)
        def _():
            send_back(p).start()

    start_first(0)
    start_south(0)
    for p in range(planes):
        if p < 3:
            start_detour(p)
        if p < EAST_AHEAD:
            start_east(p)
        start_back(p)

    @pl.when(far_east)
    def _():
        for k in range(VIA):
            send_east_relay(k).start()

    @pl.when(g == 1)
    def _():
        def clear(p, carry):
            xn[p, :, :rows - FIRST, :] = jnp.zeros((3, rows - FIRST, EDGE), BF)
            xd[p, :, :rows - FIRST, :] = jnp.zeros((3, rows - FIRST, BRICK), BF)
            wd[p, :rows - FIRST, :] = jnp.zeros((rows - FIRST, BRICK), BF)
            return carry

        lax.fori_loop(0, planes, clear, 0)

    def offsets(dg, dt):
        row_at, col_at = jnp.maximum(g - dg, 0), jnp.clip(t - dt, 0, grid_cols - 1)
        return par[row_at, 0, col_at], par[row_at, 1, col_at]

    bnd[...] = band(BRICK)
    for m, (dg, dt) in ((put_own, (0, 0)), (put_west, (0, 1)), (put_north, (1, 0)), (put_corner, (1, 1)), (put_right, (0, -1))):
        oy, ox = offsets(dg, dt)
        m[0] = onehot((BRICK, BRICK), oy)
        m[1] = onehot((BRICK, BRICK), oy - CUT)
        m[2] = onehot_cols((BRICK, BRICK), ox)
        m[3] = onehot_cols((BRICK, BRICK), ox - CUT)
    acc_w[...] = jnp.zeros_like(acc_w)
    acc_n[...] = jnp.zeros_like(acc_n)
    acc_d[...] = jnp.zeros_like(acc_d)
    acc_r[...] = jnp.zeros_like(acc_r)
    acc_b[...] = jnp.zeros_like(acc_b)

    def do_own(p):
        load_x(p).wait()
        v = x[lax.rem(p, XBUF)]
        w = content_weight(v, bnd[...])
        w_east[p] = w[:BRICK, CUT:]
        w_back[p] = w[CUT:, :BRICK]

        @pl.when(g == 0)
        def _():
            w_top[p] = w[EDGE - FIRST:EDGE - FIRST + TOP]

        @pl.when(g > 0)
        def _():
            w_top[p] = w[CUT:CUT + TOP]

        @pl.when(has_down)
        def _():
            send_top(p).start()

        @pl.when(p + 1 < planes)
        def _():
            start_first(p + 1)
            start_south(p + 1)

        @pl.when(has_right)
        def _():
            send_east_w(p).start()

        @pl.when(gives_back)
        def _():
            send_back_w(p).start()

        slot = lax.rem(p, SLOTS)
        for c in range(4):
            a = v[c] if c < 3 else w
            if c < 3:
                acc_b[c] += fold(a.astype(F32))
            left = mm(a[:BRICK, :BRICK], put_own[2]).astype(BF)
            right = mm(a[:BRICK, CUT:], put_own[3]).astype(BF)
            own[p, c] = mm(put_own[0], left).astype(BF)
            ur[slot, c] = mm(put_own[0], right).astype(BF)

        @pl.when(gets_back)
        def _():
            for c in range(4):
                a = v[c] if c < 3 else w
                lr[slot, c] = mm(put_own[1], mm(a[CUT:, CUT:], put_own[3]).astype(BF)).astype(BF)


        @pl.when(p + XBUF < planes)
        def _():
            load_x(p + XBUF).start()

    def do_west(p):
        @pl.when(has_left)
        def _():
            send_east(p).wait_recv()
            send_east_w(p).wait_recv()
            up = []
            for c in range(4):
                a = xe[p, c] if c < 3 else we[p]
                f = mm(put_west[0], mm(a, put_west[3]).astype(BF))
                west[p, c] = f.astype(BF)
                up.append(f)
            add_moments(acc_w, up, [own[p, c].astype(F32) for c in range(4)])

        @pl.when(jnp.logical_not(has_left))
        def _():
            west[p] = jnp.zeros((4, BRICK, BRICK), BF)


    def do_north(p):
        slot = lax.rem(p, SLOTS)

        @pl.when(has_up)
        def _():
            @pl.when(g == 1)
            def _():
                send_first(p).wait_recv()

            @pl.when(g > 1)
            def _():
                send_south(p).wait_recv()

            @pl.when(has_right)
            def _():
                corner_copies(p, lambda copy: copy.start())

            v = xn[p]
            wn[...] = content_weight(v, bnd[...])
            send_top(p).wait_recv()

            @pl.when(g == 1)
            def _():
                wn[rows - FIRST:rows - FIRST + TOP, :] = wt[p]

            @pl.when(g > 1)
            def _():
                wn[:TOP, :] = wt[p]

            w = wn[...]
            w_corner[p] = w[:, CUT:]

            @pl.when(has_right)
            def _():
                corner_w_copies(p, lambda copy: copy.start())

            left, right = [], []
            for c in range(4):
                a = v[c] if c < 3 else w
                f = mm(put_north[1], mm(a[:, :BRICK], put_north[2]).astype(BF))
                north[p, c] = f.astype(BF)
                left.append(f)
                right.append(mm(put_north[1], mm(a[:, CUT:], put_north[3]).astype(BF)))
            add_moments(acc_n, left, [own[p, c].astype(F32) for c in range(4)])
            add_moments(acc_n, right, [ur[slot, c].astype(F32) for c in range(4)])

        @pl.when(jnp.logical_not(has_up))
        def _():
            north[p] = jnp.zeros((4, BRICK, BRICK), BF)


    def do_corner(p):
        @pl.when(has_diag)
        def _():
            corner_copies(p, lambda copy: copy.wait_recv())
            corner_w_copies(p, lambda copy: copy.wait_recv())
            low = []
            for c in range(4):
                a = xd[p, c] if c < 3 else wd[p]
                f = mm(put_corner[1], mm(a, put_corner[3]).astype(BF))
                corner[p, c] = f.astype(BF)
                low.append(f)
            add_moments(acc_d, low, [north[p, c].astype(F32) for c in range(4)])

        @pl.when(jnp.logical_not(has_diag))
        def _():
            corner[p] = jnp.zeros((4, BRICK, BRICK), BF)


    def do_back(p):
        slot = lax.rem(p, SLOTS)

        @pl.when(gets_back)
        def _():
            send_back(p).wait_recv()
            send_back_w(p).wait_recv()
            other = []
            for c in range(4):
                a = xr[p, c] if c < 3 else wr[p]
                other.append(mm(put_right[1], mm(a, put_right[2]).astype(BF)))
            add_moments(acc_r, [lr[slot, c].astype(F32) for c in range(4)], other)

    def step(q, carry):
        p = q - LEAD

        @pl.when(q < planes)
        def _():
            do_own(q)

            @pl.when(q + EAST_AHEAD < planes)
            def _():
                start_east(q + EAST_AHEAD)

        @pl.when((p >= 0) & (p < planes))
        def _():
            do_north(p)

            for k in range(3):
                @pl.when(p == k + 1)
                def _():
                    pass_on(k)

            for k in range(VIA):
                @pl.when((p == k + 2) & lends)
                def _():
                    send_east_relay(k).wait_recv()
                    forward_east(k).start()


        @pl.when((p >= LAG) & (p < planes + LAG))
        def _():
            do_west(p - LAG)
            do_back(p - LAG)

        @pl.when((p >= LAG + 1) & (p < planes + LAG + 1))
        def _():
            do_corner(p - LAG - 1)

        return carry

    lax.fori_loop(0, planes + LEAD + LAG + 1, step, 0)

    total = put_sums(acc_d[...], 40, 2) + put_sums(acc_w[...], 0, 2) + put_sums(acc_n[...], 20, 2) + put_sums(acc_r[...], 60, 2) + put_sums(acc_b[...], 80)
    first = lax.broadcasted_iota(jnp.int32, (8, 128), 0) == 0
    row[...] = jnp.where(first, total, 0.0)

    def along_tile(d):
        return remote(row, row_buf.at[t], g1_s.at[d], g1_r.at[d], {"tile": lax.rem(t + d, grid_cols)})

    def along_grp(d):
        return remote(row_buf, all_buf.at[g], g2_s.at[d], g2_r.at[d], {"grp": lax.rem(g + d, grid_rows)})

    for d in range(1, grid_cols):
        along_tile(d).start()
    row_buf[t] = row[...]
    for d in range(1, grid_cols):
        along_tile(d).wait_recv()
    for d in range(1, grid_rows):
        along_grp(d).start()
    all_buf[g] = row_buf[...]
    for d in range(1, grid_rows):
        along_grp(d).wait_recv()
    all_out[...] = all_buf[...]

    for d in range(1, grid_cols):
        along_tile(d).wait_send()
    for d in range(1, grid_rows):
        along_grp(d).wait_send()

    def finish(p, carry):
        @pl.when(g == 0)
        def _():
            send_first(p).wait_send()

        @pl.when(has_down & (g > 0))
        def _():
            send_south(p).wait_send()

        @pl.when(has_down)
        def _():
            send_top(p).wait_send()

        @pl.when(has_right)
        def _():
            send_east(p).wait_send()
            send_east_w(p).wait_send()

        @pl.when(gives_back)
        def _():
            send_back(p).wait_send()
            send_back_w(p).wait_send()

        @pl.when(has_right & has_up)
        def _():
            corner_copies(p, lambda copy: copy.wait_send())
            corner_w_copies(p, lambda copy: copy.wait_send())

        return carry

    lax.fori_loop(0, planes, finish, 0)
    for k in range(3):
        passed_on(k)

    @pl.when(lends)
    def _():
        for k in range(VIA):
            forward_east(k).wait_send()


def gains(cols, all_ref, gain_ref, shift_ref):
    tiles = all_ref.shape[0]
    me = lax.axis_index("grp") * cols + lax.axis_index("tile")
    v = jnp.sum(all_ref[...], axis=1)

    def lanes_from(a, lane):
        return a if lane == 0 else pltpu.roll(a, 128 - lane, 1)

    east = pltpu.roll(v, tiles - 1, 0) + lanes_from(pltpu.roll(v, tiles - cols - 1, 0), 40) + lanes_from(v, 60)
    ahead = east + lanes_from(pltpu.roll(v, tiles - cols, 0), 20)
    behind = pltpu.roll(east, 1, 0) + lanes_from(v, 20)
    own_sq = ahead + lanes_from(behind, 3)
    cross = lanes_from(ahead + behind, 6)
    own_sum = lanes_from(ahead, 9) + lanes_from(behind, 12)
    other_sum = lanes_from(ahead, 12) + lanes_from(behind, 9)
    pixel_weight = lanes_from(ahead + behind, 15)
    bright = lanes_from(v, 80)
    raw = cross / own_sq
    off = (other_sum - raw * own_sum) / pixel_weight
    scale = jnp.sum(raw * bright, axis=0, keepdims=True) / jnp.sum(bright, axis=0, keepdims=True)
    rows = lax.broadcasted_iota(jnp.int32, (tiles, 128), 0)
    for k, back in enumerate((0, 1, cols, cols + 1)):
        here = rows == me - back
        gain_ref[k:k + 1] = jnp.sum(jnp.where(here, raw, 0.0), axis=0, keepdims=True) / scale
        shift_ref[k:k + 1] = jnp.sum(jnp.where(here, off, 0.0), axis=0, keepdims=True) / scale


def join_kernel(cols, all_ref, own, west, north, corner, out, gain_ref, shift_ref):
    p = pl.program_id(0)

    @pl.when(p == 0)
    def _():
        gains(cols, all_ref, gain_ref, shift_ref)

    pieces = (own, west, north, corner)
    gain = [[jnp.broadcast_to(gain_ref[k:k + 1, c:c + 1], (STRIP, 128)) for c in range(3)] for k in range(4)]
    shift = [[jnp.broadcast_to(shift_ref[k:k + 1, c:c + 1], (STRIP, 128)) for c in range(3)] for k in range(4)]

    def strip(i, carry):
        at = pl.ds(pl.multiple_of(i * STRIP, STRIP), STRIP)
        for half in range(0, BRICK, 128):
            lanes = slice(half, half + 128)
            weights = [a[p, 3, at, lanes].astype(F32) for a in pieces]
            inv = 1.0 / (weights[0] + weights[1] + weights[2] + weights[3])
            for c in range(3):
                total = None
                for k, a in enumerate(pieces):
                    term = weights[k] * (gain[k][c] * a[p, c, at, lanes].astype(F32) + shift[k][c])
                    total = term if total is None else total + term
                out[c, 0, at, lanes] = total * inv
        return carry

    lax.fori_loop(0, BRICK // STRIP, strip, 0, unroll=2)


def local(grid_rows, grid_cols, tile_stack, tile_offsets):
    x = tile_stack[0, 0]
    planes = x.shape[1]
    rows = EDGE - CUT
    tiles = grid_rows * grid_cols
    quad = pltpu.VMEM((planes, 4, BRICK, BRICK), BF)
    vmem_spec = pl.BlockSpec(memory_space=pltpu.VMEM)
    any_spec = pl.BlockSpec(memory_space=pl.ANY)

    def vmem(*shape):
        return pltpu.VMEM(shape, BF)

    def dma(*shape):
        return pltpu.SemaphoreType.DMA(shape)

    own, west, north, corner, everyone = pl.pallas_call(
        functools.partial(tile_kernel, grid_rows, grid_cols),
        out_shape=(quad,) * 4 + (pltpu.VMEM((grid_rows, grid_cols, 8, 128), F32),),
        in_specs=[pl.BlockSpec(memory_space=pltpu.SMEM), any_spec],
        out_specs=(vmem_spec,) * 5,
        scratch_shapes=[vmem(XBUF, 3, EDGE, EDGE)]
        + [
            vmem(SLOTS, 4, BRICK, BRICK),
            vmem(SLOTS, 4, BRICK, BRICK),
            vmem(planes, 3, rows, EDGE),
            vmem(planes, TOP, EDGE),
            vmem(planes, TOP, EDGE),
            vmem(rows, EDGE),
            vmem(VIA, 3, BRICK, BRICK),
            vmem(planes, 3, BRICK, BRICK),
            vmem(planes, BRICK, BRICK),
            vmem(planes, 3, BRICK, BRICK),
            vmem(planes, BRICK, BRICK),
            vmem(planes, BRICK, BRICK),
            vmem(planes, BRICK, BRICK),
            vmem(planes, 3, BRICK, BRICK),
            vmem(planes, BRICK, BRICK),
            vmem(planes, BRICK, BRICK),
            vmem(3, 3, rows, EDGE),
            vmem(BRICK, BRICK),
            vmem(4, BRICK, BRICK),
            vmem(4, BRICK, BRICK),
            vmem(4, BRICK, BRICK),
            vmem(4, BRICK, BRICK),
            vmem(4, BRICK, BRICK),
            pltpu.VMEM((16, 8, BRICK), F32),
            pltpu.VMEM((16, 8, BRICK), F32),
            pltpu.VMEM((16, 8, BRICK), F32),
            pltpu.VMEM((16, 8, BRICK), F32),
            pltpu.VMEM((8, 8, EDGE), F32),
            pltpu.VMEM((8, 128), F32),
            pltpu.VMEM((grid_cols, 8, 128), F32),
            pltpu.VMEM((grid_rows, grid_cols, 8, 128), F32),
            dma(planes),
        ]
        + [dma(planes)] * 14
        + [dma(3)] * 2
        + [dma(planes)] * 2
        + [dma(VIA)] * 2
        + [dma(grid_cols)] * 2
        + [dma(grid_rows)] * 2,
        compiler_params=pltpu.CompilerParams(collective_id=0, has_side_effects=True, vmem_limit_bytes=43 << 20),
        cost_estimate=pl.CostEstimate(flops=int(4e10), bytes_accessed=int(4e7), transcendentals=0),
    )(jnp.swapaxes(tile_offsets, 1, 2), x)

    return pl.pallas_call(
        functools.partial(join_kernel, grid_cols),
        out_shape=jax.ShapeDtypeStruct((3, planes, BRICK, BRICK), F32),
        grid=(planes,),
        in_specs=[vmem_spec] * 5,
        out_specs=pl.BlockSpec((3, 1, BRICK, BRICK), lambda i: (0, i, 0, 0)),
        scratch_shapes=[pltpu.VMEM((8, 128), F32), pltpu.VMEM((8, 128), F32)],
        compiler_params=pltpu.CompilerParams(dimension_semantics=("arbitrary",), vmem_limit_bytes=16 << 20),
        cost_estimate=pl.CostEstimate(flops=int(1e8), bytes_accessed=int(2.3e7), transcendentals=0),
    )(everyone.reshape(tiles, 8, 128), own, west, north, corner)


def solution(mesh):
    return jax.shard_map(
        functools.partial(local, mesh.shape["grp"], mesh.shape["tile"]),
        mesh=mesh,
        in_specs=(P("grp", "tile", None, None, None, None), P()),
        out_specs=P(None, None, "grp", "tile"),
        check_vma=False,
    )
```

```python
import functools

import jax
import jax.numpy as jnp
from jax import lax
from jax.experimental import pallas as pl
from jax.experimental.pallas import tpu as pltpu
from jax.sharding import PartitionSpec as P

EDGE = 384
BRICK = 256
CUT = 128
TOP = 16
STRIP = 16
VIA = 3
EAST_AHEAD = 3
LEAD = 3
LAG = 1
XBUF = 4
SLOTS = 6
FIRST = 128

half_width = 7
inv_area = 1.0 / 225.0
weight_floor = 0.1

BF = jnp.bfloat16
F32 = jnp.float32


def mm(a, b):
    return jnp.dot(a, b, preferred_element_type=F32)


def onehot(shape, shift):
    rows = lax.broadcasted_iota(jnp.int32, shape, 0)
    cols = lax.broadcasted_iota(jnp.int32, shape, 1)
    return (rows == cols + shift).astype(F32).astype(BF)


def onehot_cols(shape, shift):
    rows = lax.broadcasted_iota(jnp.int32, shape, 0)
    cols = lax.broadcasted_iota(jnp.int32, shape, 1)
    return (cols == rows + shift).astype(F32).astype(BF)


def band(edge):
    rows = lax.broadcasted_iota(jnp.int32, (edge, edge), 0)
    cols = lax.broadcasted_iota(jnp.int32, (edge, edge), 1)
    return (jnp.abs(rows - cols) <= half_width).astype(F32).astype(BF)


def box(x, bnd):
    r = x[0].shape[0]
    low = lax.broadcasted_iota(jnp.int32, (r, 128), 1) < 64
    out = []
    for v in x:
        p = mm(v[:, :256], bnd)
        q = mm(v[:, 128:], bnd)
        across = jnp.concatenate([p[:, :128], jnp.where(low, p[:, 128:], q[:, :128]), q[:, 128:]], axis=1).astype(BF)
        if r == 256:
            out.append(mm(bnd, across) * inv_area)
            continue
        top = mm(bnd[:192], across[:256])
        bottom = mm(bnd[64:], across[128:])
        out.append(jnp.concatenate([top, bottom], axis=0) * inv_area)
    return out


def content_weight(x, bnd):
    x = [x[i] for i in range(3)]
    mean = box(x, bnd)
    spread = []
    for i in range(3):
        d = x[i].astype(F32) - mean[i]
        spread.append((d * d).astype(BF))
    var = box(spread, bnd)
    return (weight_floor + (var[0] + var[1] + var[2]) / 3.0).astype(BF)


def put_sums(acc, base, spread=0):
    n, _, width = acc.shape
    part = jnp.sum(acc, axis=1)
    part = sum(part[:, k:k + 128] for k in range(0, width, 128))
    total = jnp.sum(part, axis=1, keepdims=True)
    lanes = lax.broadcasted_iota(jnp.int32, (n, 128), 1) - base
    here = lax.broadcasted_iota(jnp.int32, (n, 128), 0)
    mine = (lanes == here) | ((here == n - 1) & (lanes >= n) & (lanes < n + spread))
    return jnp.sum(jnp.where(mine, total, 0.0), axis=0, keepdims=True)


def fold(a):
    r, c = a.shape
    return jnp.sum(a.reshape(r // 8, 8, c), axis=0)


def add_moments(acc, src, dst):
    pi = src[3] * dst[3]
    for c in range(3):
        ws = src[c] * pi
        wd = dst[c] * pi
        acc[0 + c] += fold(ws * src[c])
        acc[3 + c] += fold(wd * dst[c])
        acc[6 + c] += fold(ws * dst[c])
        acc[9 + c] += fold(ws)
        acc[12 + c] += fold(wd)
    acc[15] += fold(pi)


def tile_kernel(
    grid_rows, grid_cols, par, x_hbm,
    own, west, north, corner, all_out,
    x, ur,
    lr, xn, w_top, wt, wn, relay_e, xe, we, xd, wd, w_east, w_corner, xr, wr, w_back, relay,
    bnd, put_own, put_west, put_north, put_corner, put_right,
    acc_w, acc_n, acc_d, acc_r, acc_b, row, row_buf, all_buf,
    x_sem, sn_s, sn_r, ex_s, ex_r, ew_s, ew_r, cx_s, cx_r, cw_s, cw_r, bx_s, bx_r, bw_s, bw_r,
    rl_r, fw_s, tp_s, tp_r, re_r, fe_s, lp_s, lp_r, g1_s, g1_r, g2_s, g2_r,
):
    planes = own.shape[0]
    rows = EDGE - CUT
    g, t = lax.axis_index("grp"), lax.axis_index("tile")
    has_right, has_down = t < grid_cols - 1, g < grid_rows - 1
    has_left, has_up = t > 0, g > 0
    has_diag = has_left & has_up
    is_last = g == grid_rows - 1
    gets_back, gives_back = is_last & has_right, is_last & has_left
    detours = grid_rows == 4
    to_right = {"tile": lax.rem(t + 1, grid_cols)}
    to_down = {"grp": lax.rem(g + 1, grid_rows)}
    to_left = {"tile": lax.rem(t + grid_cols - 1, grid_cols)}

    def remote(src, dst, send, recv, to):
        return pltpu.make_async_remote_copy(
            src_ref=src, dst_ref=dst, send_sem=send, recv_sem=recv, device_id=to, device_id_type=pl.DeviceIdType.MESH
        )

    def load_x(p):
        return pltpu.make_async_copy(x_hbm.at[:, p], x.at[lax.rem(p, XBUF)], x_sem.at[p])

    def send_south(p):
        return remote(x_hbm.at[:, p, pl.ds(CUT, rows), :], xn.at[p], sn_s.at[p], sn_r.at[p], to_down)

    def send_first(p):
        return remote(
            x_hbm.at[:, p, pl.ds(EDGE - FIRST, FIRST), :], xn.at[p, :, pl.ds(rows - FIRST, FIRST), :],
            sn_s.at[p], sn_r.at[p], to_down,
        )

    def send_relay(p, slot, via):
        return remote(x_hbm.at[:, p, pl.ds(CUT, rows), :], relay.at[slot], sn_s.at[p], rl_r.at[slot], {"grp": via})

    def forward(p, slot, to):
        return remote(relay.at[slot], xn.at[p], fw_s.at[slot], sn_r.at[p], {"grp": to})

    def detour(p):
        if not detours:
            return g < 0
        by_last = (g == 1) & ((p == 2) | (p == 4) | (p == 6))
        by_first = (g == 2) & ((p == 4) | (p == 6))
        return by_last | by_first

    def start_detour(slot):
        if not detours:
            return
        if slot < 3:
            @pl.when(g == 1)
            def _():
                send_relay(2 + 2 * slot, slot, 3).start()
        if slot < 2:
            @pl.when(g == 2)
            def _():
                send_relay(4 + 2 * slot, slot, 0).start()

    def pass_on(slot):
        if not detours:
            return
        if slot < 3:
            @pl.when(g == 3)
            def _():
                send_relay(2 + 2 * slot, slot, 1).wait_recv()
                forward(2 + 2 * slot, slot, 2).start()
        if slot < 2:
            @pl.when(g == 0)
            def _():
                send_relay(4 + 2 * slot, slot, 1).wait_recv()
                forward(4 + 2 * slot, slot, 3).start()

    def passed_on(slot):
        if not detours:
            return
        if slot < 3:
            @pl.when(g == 3)
            def _():
                forward(2 + 2 * slot, slot, 2).wait_send()
        if slot < 2:
            @pl.when(g == 0)
            def _():
                forward(4 + 2 * slot, slot, 3).wait_send()

    def send_back(p):
        return remote(x_hbm.at[:, p, pl.ds(CUT, BRICK), pl.ds(0, BRICK)], xr.at[p], bx_s.at[p], bx_r.at[p], to_left)

    def send_back_w(p):
        return remote(w_back.at[p], wr.at[p], bw_s.at[p], bw_r.at[p], to_left)

    def send_east(p):
        return remote(x_hbm.at[:, p, pl.ds(0, BRICK), pl.ds(CUT, BRICK)], xe.at[p], ex_s.at[p], ex_r.at[p], to_right)

    def send_east_w(p):
        return remote(w_east.at[p], we.at[p], ew_s.at[p], ew_r.at[p], to_right)

    def send_corner(p):
        return remote(xn.at[p, :, :, pl.ds(CUT, BRICK)], xd.at[p], cx_s.at[p], cx_r.at[p], to_right)

    def send_corner_w(p):
        return remote(w_corner.at[p], wd.at[p], cw_s.at[p], cw_r.at[p], to_right)

    def send_corner_low(p):
        low = pl.ds(rows - FIRST, FIRST)
        return remote(xn.at[p, :, low, pl.ds(CUT, BRICK)], xd.at[p, :, low, :], cx_s.at[p], cx_r.at[p], to_right)

    def send_corner_w_low(p):
        low = pl.ds(rows - FIRST, FIRST)
        return remote(w_corner.at[p, low, :], wd.at[p, low, :], cw_s.at[p], cw_r.at[p], to_right)

    def corner_copies(p, act):
        @pl.when(g == 1)
        def _():
            act(send_corner_low(p))

        @pl.when(g > 1)
        def _():
            act(send_corner(p))

    def corner_w_copies(p, act):
        @pl.when(g == 1)
        def _():
            act(send_corner_w_low(p))

        @pl.when(g > 1)
        def _():
            act(send_corner_w(p))

    def send_top(p):
        return remote(w_top.at[p], wt.at[p], tp_s.at[p], tp_r.at[p], to_down)

    crosses = (lax.rem(t, 2) == 1) & has_right
    far_east = crosses & (g >= 2) if detours else t < 0
    lends = (lax.rem(t, 2) == 0) & has_left & (g < 2) if detours else g < 0
    two_rows = lax.rem(g + 2, grid_rows)

    def send_east_relay(k):
        p = planes - VIA + k
        return remote(
            x_hbm.at[:, p, pl.ds(0, BRICK), pl.ds(CUT, BRICK)], relay_e.at[k], ex_s.at[p], re_r.at[k],
            {"grp": two_rows, "tile": lax.rem(t + 1, grid_cols)},
        )

    def forward_east(k):
        p = planes - VIA + k
        return remote(relay_e.at[k], xe.at[p], fe_s.at[k], ex_r.at[p], {"grp": two_rows})

    for p in range(XBUF):
        load_x(p).start()

    barrier = pltpu.get_barrier_semaphore()
    for axis, me, size in (("tile", t, grid_cols), ("grp", g, grid_rows)):
        for d in range(1, size):
            pl.semaphore_signal(
                barrier, inc=1, device_id={axis: lax.rem(me + d, size)}, device_id_type=pl.DeviceIdType.MESH
            )

    @pl.when(lends)
    def _():
        pl.semaphore_signal(
            barrier, inc=1, device_id={"grp": two_rows, "tile": lax.rem(t + grid_cols - 1, grid_cols)},
            device_id_type=pl.DeviceIdType.MESH,
        )

    @pl.when(far_east)
    def _():
        pl.semaphore_wait(barrier, grid_cols + grid_rows - 1)

    @pl.when(jnp.logical_not(far_east))
    def _():
        pl.semaphore_wait(barrier, grid_cols + grid_rows - 2)

    last = planes - 1

    def send_last(k):
        cols = (pl.ds(CUT, BRICK), pl.ds(0, CUT))[k]
        return remote(
            x_hbm.at[:, last, pl.ds(CUT, rows), cols], xn.at[last, :, :, cols], lp_s.at[k], lp_r.at[k], to_down
        )

    def send_first_last(k):
        cols = (pl.ds(CUT, BRICK), pl.ds(0, CUT))[k]
        return remote(
            x_hbm.at[:, last, pl.ds(EDGE - FIRST, FIRST), cols], xn.at[last, :, pl.ds(rows - FIRST, FIRST), cols],
            lp_s.at[k], lp_r.at[k], to_down,
        )

    def start_last(p):
        @pl.when((p == last) & (g == 0))
        def _():
            send_first_last(0).start()
            send_first_last(1).start()

        @pl.when((p == last) & has_down & (g > 0))
        def _():
            send_last(0).start()
            send_last(1).start()

    def arrive_last(p, k):
        @pl.when((p == last) & (g == 1))
        def _():
            send_first_last(k).wait_recv()

        @pl.when((p == last) & (g > 1))
        def _():
            send_last(k).wait_recv()

    def start_first(p):
        @pl.when((g == 0) & (p < last))
        def _():
            send_first(p).start()

    def start_south(p):
        @pl.when(has_down & (g > 0) & (p < last) & jnp.logical_not(detour(p)))
        def _():
            send_south(p).start()

    def start_east(p):
        @pl.when(has_right & jnp.logical_not(far_east & (p >= planes - VIA)))
        def _():
            send_east(p).start()

    def start_back(p):
        @pl.when(gives_back)
        def _():
            send_back(p).start()

    start_first(0)
    start_south(0)
    for p in range(planes):
        if p < 3:
            start_detour(p)
        if p < EAST_AHEAD:
            start_east(p)
        start_back(p)

    @pl.when(far_east)
    def _():
        for k in range(VIA):
            send_east_relay(k).start()

    @pl.when(g == 1)
    def _():
        def clear(p, carry):
            xn[p, :, :rows - FIRST, :] = jnp.zeros((3, rows - FIRST, EDGE), BF)
            xd[p, :, :rows - FIRST, :] = jnp.zeros((3, rows - FIRST, BRICK), BF)
            wd[p, :rows - FIRST, :] = jnp.zeros((rows - FIRST, BRICK), BF)
            return carry

        lax.fori_loop(0, planes, clear, 0)

    def offsets(dg, dt):
        row_at, col_at = jnp.maximum(g - dg, 0), jnp.clip(t - dt, 0, grid_cols - 1)
        return par[row_at, 0, col_at], par[row_at, 1, col_at]

    bnd[...] = band(BRICK)
    for m, (dg, dt) in ((put_own, (0, 0)), (put_west, (0, 1)), (put_north, (1, 0)), (put_corner, (1, 1)), (put_right, (0, -1))):
        oy, ox = offsets(dg, dt)
        m[0] = onehot((BRICK, BRICK), oy)
        m[1] = onehot((BRICK, BRICK), oy - CUT)
        m[2] = onehot_cols((BRICK, BRICK), ox)
        m[3] = onehot_cols((BRICK, BRICK), ox - CUT)
    acc_w[...] = jnp.zeros_like(acc_w)
    acc_n[...] = jnp.zeros_like(acc_n)
    acc_d[...] = jnp.zeros_like(acc_d)
    acc_r[...] = jnp.zeros_like(acc_r)
    acc_b[...] = jnp.zeros_like(acc_b)

    def do_own(p):
        load_x(p).wait()
        v = x[lax.rem(p, XBUF)]
        w = content_weight(v, bnd[...])
        w_east[p] = w[:BRICK, CUT:]
        w_back[p] = w[CUT:, :BRICK]

        @pl.when(g == 0)
        def _():
            w_top[p] = w[EDGE - FIRST:EDGE - FIRST + TOP]

        @pl.when(g > 0)
        def _():
            w_top[p] = w[CUT:CUT + TOP]

        @pl.when(has_down)
        def _():
            send_top(p).start()

        @pl.when(p + 1 < planes)
        def _():
            start_first(p + 1)
            start_south(p + 1)
            start_last(p + 1)

        @pl.when(has_right)
        def _():
            send_east_w(p).start()

        @pl.when(gives_back)
        def _():
            send_back_w(p).start()

        slot = lax.rem(p, SLOTS)
        for c in range(4):
            a = v[c] if c < 3 else w
            if c < 3:
                acc_b[c] += fold(a.astype(F32))
            left = mm(a[:BRICK, :BRICK], put_own[2]).astype(BF)
            right = mm(a[:BRICK, CUT:], put_own[3]).astype(BF)
            own[p, c] = mm(put_own[0], left).astype(BF)
            ur[slot, c] = mm(put_own[0], right).astype(BF)

        @pl.when(gets_back)
        def _():
            for c in range(4):
                a = v[c] if c < 3 else w
                lr[slot, c] = mm(put_own[1], mm(a[CUT:, CUT:], put_own[3]).astype(BF)).astype(BF)


        @pl.when(p + XBUF < planes)
        def _():
            load_x(p + XBUF).start()

    def do_west(p):
        @pl.when(has_left)
        def _():
            send_east(p).wait_recv()
            send_east_w(p).wait_recv()
            up = []
            for c in range(4):
                a = xe[p, c] if c < 3 else we[p]
                f = mm(put_west[0], mm(a, put_west[3]).astype(BF))
                west[p, c] = f.astype(BF)
                up.append(f)
            add_moments(acc_w, up, [own[p, c].astype(F32) for c in range(4)])

        @pl.when(jnp.logical_not(has_left))
        def _():
            west[p] = jnp.zeros((4, BRICK, BRICK), BF)


    def do_north(p):
        slot = lax.rem(p, SLOTS)

        @pl.when(has_up)
        def _():
            @pl.when((g == 1) & (p < last))
            def _():
                send_first(p).wait_recv()

            @pl.when((g > 1) & (p < last))
            def _():
                send_south(p).wait_recv()

            arrive_last(p, 0)

            @pl.when(has_right)
            def _():
                corner_copies(p, lambda copy: copy.start())

            arrive_last(p, 1)

            v = xn[p]
            wn[...] = content_weight(v, bnd[...])
            send_top(p).wait_recv()

            @pl.when(g == 1)
            def _():
                wn[rows - FIRST:rows - FIRST + TOP, :] = wt[p]

            @pl.when(g > 1)
            def _():
                wn[:TOP, :] = wt[p]

            w = wn[...]
            w_corner[p] = w[:, CUT:]

            @pl.when(has_right)
            def _():
                corner_w_copies(p, lambda copy: copy.start())

            left, right = [], []
            for c in range(4):
                a = v[c] if c < 3 else w
                f = mm(put_north[1], mm(a[:, :BRICK], put_north[2]).astype(BF))
                north[p, c] = f.astype(BF)
                left.append(f)
                right.append(mm(put_north[1], mm(a[:, CUT:], put_north[3]).astype(BF)))
            add_moments(acc_n, left, [own[p, c].astype(F32) for c in range(4)])
            add_moments(acc_n, right, [ur[slot, c].astype(F32) for c in range(4)])

        @pl.when(jnp.logical_not(has_up))
        def _():
            north[p] = jnp.zeros((4, BRICK, BRICK), BF)


    def do_corner(p):
        @pl.when(has_diag)
        def _():
            corner_copies(p, lambda copy: copy.wait_recv())
            corner_w_copies(p, lambda copy: copy.wait_recv())
            low = []
            for c in range(4):
                a = xd[p, c] if c < 3 else wd[p]
                f = mm(put_corner[1], mm(a, put_corner[3]).astype(BF))
                corner[p, c] = f.astype(BF)
                low.append(f)
            add_moments(acc_d, low, [north[p, c].astype(F32) for c in range(4)])

        @pl.when(jnp.logical_not(has_diag))
        def _():
            corner[p] = jnp.zeros((4, BRICK, BRICK), BF)


    def do_back(p):
        slot = lax.rem(p, SLOTS)

        @pl.when(gets_back)
        def _():
            send_back(p).wait_recv()
            send_back_w(p).wait_recv()
            other = []
            for c in range(4):
                a = xr[p, c] if c < 3 else wr[p]
                other.append(mm(put_right[1], mm(a, put_right[2]).astype(BF)))
            add_moments(acc_r, [lr[slot, c].astype(F32) for c in range(4)], other)

    def step(q, carry):
        p = q - LEAD

        @pl.when(q < planes)
        def _():
            do_own(q)

            @pl.when(q + EAST_AHEAD < planes)
            def _():
                start_east(q + EAST_AHEAD)

        @pl.when((p >= 0) & (p < planes))
        def _():
            do_north(p)

            for k in range(3):
                @pl.when(p == k + 1)
                def _():
                    pass_on(k)

            for k in range(VIA):
                @pl.when((p == k + 2) & lends)
                def _():
                    send_east_relay(k).wait_recv()
                    forward_east(k).start()


        @pl.when((p >= LAG) & (p < planes + LAG))
        def _():
            do_west(p - LAG)
            do_back(p - LAG)

        @pl.when((p >= LAG + 1) & (p < planes + LAG + 1))
        def _():
            do_corner(p - LAG - 1)

        return carry

    lax.fori_loop(0, planes + LEAD + LAG + 1, step, 0)

    total = put_sums(acc_d[...], 40, 2) + put_sums(acc_w[...], 0, 2) + put_sums(acc_n[...], 20, 2) + put_sums(acc_r[...], 60, 2) + put_sums(acc_b[...], 80)
    first = lax.broadcasted_iota(jnp.int32, (8, 128), 0) == 0
    row[...] = jnp.where(first, total, 0.0)

    def along_tile(d):
        return remote(row, row_buf.at[t], g1_s.at[d], g1_r.at[d], {"tile": lax.rem(t + d, grid_cols)})

    def along_grp(d):
        return remote(row_buf, all_buf.at[g], g2_s.at[d], g2_r.at[d], {"grp": lax.rem(g + d, grid_rows)})

    for d in range(1, grid_cols):
        along_tile(d).start()
    row_buf[t] = row[...]
    for d in range(1, grid_cols):
        along_tile(d).wait_recv()
    for d in range(1, grid_rows):
        along_grp(d).start()
    all_buf[g] = row_buf[...]
    for d in range(1, grid_rows):
        along_grp(d).wait_recv()
    all_out[...] = all_buf[...]

    for d in range(1, grid_cols):
        along_tile(d).wait_send()
    for d in range(1, grid_rows):
        along_grp(d).wait_send()

    def finish(p, carry):
        @pl.when((g == 0) & (p < last))
        def _():
            send_first(p).wait_send()

        @pl.when(has_down & (g > 0) & (p < last))
        def _():
            send_south(p).wait_send()

        @pl.when(has_down)
        def _():
            send_top(p).wait_send()

        @pl.when(has_right)
        def _():
            send_east(p).wait_send()
            send_east_w(p).wait_send()

        @pl.when(gives_back)
        def _():
            send_back(p).wait_send()
            send_back_w(p).wait_send()

        @pl.when(has_right & has_up)
        def _():
            corner_copies(p, lambda copy: copy.wait_send())
            corner_w_copies(p, lambda copy: copy.wait_send())

        return carry

    lax.fori_loop(0, planes, finish, 0)

    @pl.when(g == 0)
    def _():
        for k in range(2):
            send_first_last(k).wait_send()

    @pl.when(has_down & (g > 0))
    def _():
        for k in range(2):
            send_last(k).wait_send()

    for k in range(3):
        passed_on(k)

    @pl.when(lends)
    def _():
        for k in range(VIA):
            forward_east(k).wait_send()


def gains(cols, all_ref, gain_ref, shift_ref):
    tiles = all_ref.shape[0]
    me = lax.axis_index("grp") * cols + lax.axis_index("tile")
    v = jnp.sum(all_ref[...], axis=1)

    def lanes_from(a, lane):
        return a if lane == 0 else pltpu.roll(a, 128 - lane, 1)

    east = pltpu.roll(v, tiles - 1, 0) + lanes_from(pltpu.roll(v, tiles - cols - 1, 0), 40) + lanes_from(v, 60)
    ahead = east + lanes_from(pltpu.roll(v, tiles - cols, 0), 20)
    behind = pltpu.roll(east, 1, 0) + lanes_from(v, 20)
    own_sq = ahead + lanes_from(behind, 3)
    cross = lanes_from(ahead + behind, 6)
    own_sum = lanes_from(ahead, 9) + lanes_from(behind, 12)
    other_sum = lanes_from(ahead, 12) + lanes_from(behind, 9)
    pixel_weight = lanes_from(ahead + behind, 15)
    bright = lanes_from(v, 80)
    raw = cross / own_sq
    off = (other_sum - raw * own_sum) / pixel_weight
    scale = jnp.sum(raw * bright, axis=0, keepdims=True) / jnp.sum(bright, axis=0, keepdims=True)
    rows = lax.broadcasted_iota(jnp.int32, (tiles, 128), 0)
    for k, back in enumerate((0, 1, cols, cols + 1)):
        here = rows == me - back
        gain_ref[k:k + 1] = jnp.sum(jnp.where(here, raw, 0.0), axis=0, keepdims=True) / scale
        shift_ref[k:k + 1] = jnp.sum(jnp.where(here, off, 0.0), axis=0, keepdims=True) / scale


def join_kernel(cols, all_ref, own, west, north, corner, out, gain_ref, shift_ref):
    p = pl.program_id(0)

    @pl.when(p == 0)
    def _():
        gains(cols, all_ref, gain_ref, shift_ref)

    pieces = (own, west, north, corner)
    gain = [[jnp.broadcast_to(gain_ref[k:k + 1, c:c + 1], (STRIP, 128)) for c in range(3)] for k in range(4)]
    shift = [[jnp.broadcast_to(shift_ref[k:k + 1, c:c + 1], (STRIP, 128)) for c in range(3)] for k in range(4)]

    def strip(i, carry):
        at = pl.ds(pl.multiple_of(i * STRIP, STRIP), STRIP)
        for half in range(0, BRICK, 128):
            lanes = slice(half, half + 128)
            weights = [a[p, 3, at, lanes].astype(F32) for a in pieces]
            inv = 1.0 / (weights[0] + weights[1] + weights[2] + weights[3])
            for c in range(3):
                total = None
                for k, a in enumerate(pieces):
                    term = weights[k] * (gain[k][c] * a[p, c, at, lanes].astype(F32) + shift[k][c])
                    total = term if total is None else total + term
                out[c, 0, at, lanes] = total * inv
        return carry

    lax.fori_loop(0, BRICK // STRIP, strip, 0, unroll=2)


def local(grid_rows, grid_cols, tile_stack, tile_offsets):
    x = tile_stack[0, 0]
    planes = x.shape[1]
    rows = EDGE - CUT
    tiles = grid_rows * grid_cols
    quad = pltpu.VMEM((planes, 4, BRICK, BRICK), BF)
    vmem_spec = pl.BlockSpec(memory_space=pltpu.VMEM)
    any_spec = pl.BlockSpec(memory_space=pl.ANY)

    def vmem(*shape):
        return pltpu.VMEM(shape, BF)

    def dma(*shape):
        return pltpu.SemaphoreType.DMA(shape)

    own, west, north, corner, everyone = pl.pallas_call(
        functools.partial(tile_kernel, grid_rows, grid_cols),
        out_shape=(quad,) * 4 + (pltpu.VMEM((grid_rows, grid_cols, 8, 128), F32),),
        in_specs=[pl.BlockSpec(memory_space=pltpu.SMEM), any_spec],
        out_specs=(vmem_spec,) * 5,
        scratch_shapes=[vmem(XBUF, 3, EDGE, EDGE)]
        + [
            vmem(SLOTS, 4, BRICK, BRICK),
            vmem(SLOTS, 4, BRICK, BRICK),
            vmem(planes, 3, rows, EDGE),
            vmem(planes, TOP, EDGE),
            vmem(planes, TOP, EDGE),
            vmem(rows, EDGE),
            vmem(VIA, 3, BRICK, BRICK),
            vmem(planes, 3, BRICK, BRICK),
            vmem(planes, BRICK, BRICK),
            vmem(planes, 3, BRICK, BRICK),
            vmem(planes, BRICK, BRICK),
            vmem(planes, BRICK, BRICK),
            vmem(planes, BRICK, BRICK),
            vmem(planes, 3, BRICK, BRICK),
            vmem(planes, BRICK, BRICK),
            vmem(planes, BRICK, BRICK),
            vmem(3, 3, rows, EDGE),
            vmem(BRICK, BRICK),
            vmem(4, BRICK, BRICK),
            vmem(4, BRICK, BRICK),
            vmem(4, BRICK, BRICK),
            vmem(4, BRICK, BRICK),
            vmem(4, BRICK, BRICK),
            pltpu.VMEM((16, 8, BRICK), F32),
            pltpu.VMEM((16, 8, BRICK), F32),
            pltpu.VMEM((16, 8, BRICK), F32),
            pltpu.VMEM((16, 8, BRICK), F32),
            pltpu.VMEM((8, 8, EDGE), F32),
            pltpu.VMEM((8, 128), F32),
            pltpu.VMEM((grid_cols, 8, 128), F32),
            pltpu.VMEM((grid_rows, grid_cols, 8, 128), F32),
            dma(planes),
        ]
        + [dma(planes)] * 14
        + [dma(3)] * 2
        + [dma(planes)] * 2
        + [dma(VIA)] * 2
        + [dma(2)] * 2
        + [dma(grid_cols)] * 2
        + [dma(grid_rows)] * 2,
        compiler_params=pltpu.CompilerParams(collective_id=0, has_side_effects=True, vmem_limit_bytes=43 << 20),
        cost_estimate=pl.CostEstimate(flops=int(4e10), bytes_accessed=int(4e7), transcendentals=0),
    )(jnp.swapaxes(tile_offsets, 1, 2), x)

    return pl.pallas_call(
        functools.partial(join_kernel, grid_cols),
        out_shape=jax.ShapeDtypeStruct((3, planes, BRICK, BRICK), F32),
        grid=(planes,),
        in_specs=[vmem_spec] * 5,
        out_specs=pl.BlockSpec((3, 1, BRICK, BRICK), lambda i: (0, i, 0, 0)),
        scratch_shapes=[pltpu.VMEM((8, 128), F32), pltpu.VMEM((8, 128), F32)],
        compiler_params=pltpu.CompilerParams(dimension_semantics=("arbitrary",), vmem_limit_bytes=16 << 20),
        cost_estimate=pl.CostEstimate(flops=int(1e8), bytes_accessed=int(2.3e7), transcendentals=0),
    )(everyone.reshape(tiles, 8, 128), own, west, north, corner)


def solution(mesh):
    return jax.shard_map(
        functools.partial(local, mesh.shape["grp"], mesh.shape["tile"]),
        mesh=mesh,
        in_specs=(P("grp", "tile", None, None, None, None), P()),
        out_specs=P(None, None, "grp", "tile"),
        check_vma=False,
    )
```
